32 devices in a mesh: groups: 2 (over x), chan: 16 (over z, y, core).
Axes of the slice: x: 2, y: 2, z: 4, core: 2. Of those that a mesh axis runs over, the one named last changes fastest.
Arguments:
- waveforms: bfloat16 [10240, 15360], P('chan', 'groups'), parts along dimension 1, may hold values from -250 to 250
- basis: bfloat16 [16, 10240, 200], P(None, 'chan'), may hold values from -1 to 1
- bounds: int32 [2, 768], replicated, may hold values from 0 to 5120, as said below
Outputs:
- detection: float32 [15360], P(('groups', 'chan')), parts along dimension 0
- coefficients: float32 [16, 15360], P(None, ('groups', 'chan')), parts along dimension 1
The draws below stay inside these ranges and needn't reach their ends.
There are 2 independent parts, one for each index of `groups`. The reference program is written for one: setup_inputs(seed, part) draws one part's arguments, and reference() takes and returns one part's arrays. A program takes and returns all parts, laid end to end along the dimension named above; an argument that names none is the same for every part. Nothing has to cross between parts.
Inputs may be any that keep to these rules, and one draw needn't show every extreme that they name: bounds[0, 0] is 0 and every bounds[0, f] is below 160; bounds[1, f] grows roughly in proportion to f and is 5120 at the last bin; where bounds[0, f] exceeds bounds[1, f] nothing passes.
All inputs are finite; a program needn't handle non-finite values.
Results may differ from the reference program's by a relative error of at most 0.017.
Values may be sent and summed in bfloat16 or wider, within the bound.
A program may use at most 128 MiB of HBM per device.

```python
import math
import jax
import jax.numpy as jnp
from jax import lax

C = 10240
FRAME_SPAN = 7680
F = 768
R = 16
L = 200


def draw_waveforms(key, part):
    noise_key, scale_key = jax.random.split(key, 2)
    channel_ramp = 1.0 + 2.0 * jnp.arange(C, dtype=jnp.float32) / C
    spread = jnp.exp(jax.random.uniform(scale_key, (C, 1), jnp.float32, 0.0, math.log(10.0)))
    background_clutter = jnp.clip(jax.random.normal(noise_key, (C, FRAME_SPAN), jnp.float32), -5.0, 5.0)
    return (background_clutter * spread * channel_ramp[:, None]).astype(jnp.bfloat16)


def draw_basis(key, part):
    noise_key, scale_key = jax.random.split(jax.random.fold_in(key, 7), 2)
    raw_noise = jnp.clip(jax.random.normal(noise_key, (R, C, L), jnp.float32), -5.0, 5.0)
    mixed_taps = raw_noise + 0.6 * jnp.roll(raw_noise, 1, axis=0)
    channel_ramp = 1.0 + 2.0 * jnp.arange(C, dtype=jnp.float32) / C
    amplitude = jnp.exp(jax.random.uniform(scale_key, (1, C, 1), jnp.float32, 0.0, math.log(4.0)))
    amplitude = amplitude * channel_ramp[None, :, None]
    return (mixed_taps * amplitude / (3.0 * jnp.sqrt(jnp.float32(C * L)))).astype(jnp.bfloat16)


def draw_bounds(key, part):
    low_key, high_key = jax.random.split(jax.random.fold_in(key, 11), 2)
    slot_indices = jnp.arange(F, dtype=jnp.int32)
    half_count = C // 2
    upper_edge = jnp.minimum(half_count, (slot_indices + 1) * half_count // F + jax.random.randint(high_key, (F,), 0, C // 16, dtype=jnp.int32))
    lower_cutoff = jnp.where(slot_indices == 0, 0, jax.random.randint(low_key, (F,), 0, C // 64, dtype=jnp.int32))
    return jnp.stack([lower_cutoff, upper_edge]).astype(jnp.int32)


def setup_inputs(seed: int = 0, part: int = 0) -> dict:
    keys = jax.random.split(jax.random.key(seed), 4)
    part_keys = jax.random.split(jax.random.fold_in(keys[3], part), 4)
    waveforms = draw_waveforms(jax.random.fold_in(jax.random.fold_in(keys[3], part), 71), part)
    basis = draw_basis(jax.random.fold_in(keys[3], 71), part)
    bounds = draw_bounds(jax.random.fold_in(keys[3], 71), part)
    return {"waveforms": waveforms, "basis": basis, "bounds": bounds}


def settle(values):
    return lax.optimization_barrier(values.astype(jnp.bfloat16)).astype(jnp.float32)

def half_spectrum(real_part, imag_part, recorded_readings):
    slot_indices = jnp.arange(real_part.shape[-1], dtype=jnp.int32)
    imag_kept = jnp.where(slot_indices == 0, jnp.zeros_like(imag_part), imag_part)
    combined = real_part + 1j * imag_kept
    filler = jnp.zeros(real_part.shape[:-1] + (recorded_readings // 2 + 1 - real_part.shape[-1],), dtype=combined.dtype)
    return jnp.concatenate([combined, filler], axis=-1)

def reference(waveforms, basis, bounds):
    signal = waveforms.astype(jnp.float32)
    spectrum = jnp.fft.rfft(signal, axis=1)[:, :F]
    spectrum_real = settle(jnp.real(spectrum))
    spectrum_imag = settle(jnp.imag(spectrum))
    wavenumbers = jnp.fft.fft(spectrum_real + 1j * spectrum_imag, axis=0)
    wave_ids = jnp.arange(C, dtype=jnp.int32)
    magnitude = jnp.where(wave_ids > C // 2, C - wave_ids, wave_ids)[:, None]
    passing = (magnitude >= bounds[0][None, :]) & (magnitude <= bounds[1][None, :])
    passed = jnp.where(passing, wavenumbers, jnp.zeros_like(wavenumbers))
    filtered = jnp.fft.ifft(passed, axis=0)
    filtered_real = settle(jnp.real(filtered))
    filtered_imag = settle(jnp.imag(filtered))
    traces = jnp.fft.irfft(half_spectrum(filtered_real, filtered_imag, FRAME_SPAN), n=FRAME_SPAN, axis=1)
    trace_power = lax.optimization_barrier(jnp.sum(traces * traces, axis=0))
    extended = jnp.concatenate([trace_power, trace_power[:L]])
    running = jnp.concatenate([jnp.zeros((1,), extended.dtype), jnp.cumsum(extended)])
    energy = running[L:L + FRAME_SPAN] - running[:FRAME_SPAN]
    filtered_full = filtered_real + 1j * filtered_imag

    def project(subspace_vector):
        transformed = jnp.fft.rfft(subspace_vector.astype(jnp.float32), n=FRAME_SPAN, axis=1)[:, :F]
        product = jnp.conj(transformed) * filtered_full
        return jnp.stack([lax.optimization_barrier(jnp.sum(jnp.real(product), axis=0)), lax.optimization_barrier(jnp.sum(jnp.imag(product), axis=0))])
    spectra = lax.map(project, basis)
    correlation = jnp.fft.irfft(half_spectrum(spectra[:, 0], spectra[:, 1], FRAME_SPAN), n=FRAME_SPAN, axis=1)
    flattened = basis.astype(jnp.float32).reshape(R, C * L)
    gram_matrix = jnp.dot(flattened, flattened.T, precision=lax.Precision.HIGHEST)
    energy_threshold = energy / (C * L) + 1e-06
    solved = jnp.linalg.solve(gram_matrix, correlation)
    detection = lax.optimization_barrier(jnp.sum(correlation * solved, axis=0)) / (R * energy_threshold)
    coefficients = correlation / jnp.sqrt(energy_threshold)[None, :]
    return (detection, coefficients)
```

```python
import functools
import math

import jax
import jax.numpy as jnp
import numpy as np
from jax import lax
from jax.experimental import pallas as pl
from jax.experimental.pallas import tpu as pltpu
from jax.sharding import PartitionSpec as P

radix = 12
half = radix // 2
lanes = 128
highest = lax.Precision.HIGHEST
bf16 = jnp.bfloat16
f32 = jnp.float32
vmem_limit = 60 * 1024 * 1024


def even_parts(x0, x6, s):
    r = math.sqrt(3.0) / 2.0
    s1, s2, s3, s4, s5 = s
    u, v = x0 + x6, x0 - x6
    e24, d24, e15, d15 = s2 + s4, s2 - s4, s1 + s5, s1 - s5
    even0, odd0 = u + e24, e15 + s3
    even1, odd1 = v + 0.5 * d24, r * d15
    even2, odd2 = u - 0.5 * e24, 0.5 * e15 - s3
    return (
        even0 + odd0,
        even1 + odd1,
        even2 + odd2,
        v - d24,
        even2 - odd2,
        even1 - odd1,
        even0 - odd0,
    )


def odd_parts(d):
    r = math.sqrt(3.0) / 2.0
    d1, d2, d3, d4, d5 = d
    e15, m15 = d1 + d5, d1 - d5
    odd1, even1 = 0.5 * e15 + d3, r * (d2 + d4)
    odd2, even2 = r * m15, r * (d2 - d4)
    return (odd1 + even1, odd2 + even2, e15 - d3, odd2 - even2, odd1 - even1)


def bin_order(frequencies):
    ids = np.arange(frequencies)
    groups = [np.concatenate([ids[ids % radix == 0], ids[ids % radix == half]])]
    signs = [np.ones(frequencies // half)]
    for q in range(1, half):
        plus, minus = ids[ids % radix == q], ids[ids % radix == radix - q]
        groups.append(np.concatenate([plus, minus]))
        signs.append(np.concatenate([np.ones(len(plus)), -np.ones(len(minus))]))
    return np.stack(groups), np.stack(signs)


def time_table(frequencies, readings, fold):
    width = readings // radix
    groups, signs = bin_order(frequencies)
    theta = (groups[:, :, None] * np.arange(width)[None, None, :] % readings) * (
        2.0 * np.pi / readings
    )
    cos, sin = np.cos(theta), np.sin(theta)
    sg = signs[:, :, None]
    real = np.concatenate([cos, -sg * sin], axis=2)
    imag = np.concatenate([-sin, -sg * cos], axis=2)
    first = (groups[0] % radix == 0)[:, None]
    real[0] = np.concatenate([np.where(first, cos[0], 0), np.where(first, 0, cos[0])], axis=1)
    imag[0] = np.concatenate([np.where(first, -sin[0], 0), np.where(first, 0, -sin[0])], axis=1)
    count = groups.shape[1]
    both = np.stack([real, imag], axis=1).reshape(half, 2, count // fold, fold, 2 * width)
    return both.transpose(0, 2, 1, 3, 4).reshape(half, 2 * count, 2 * width)


def row_bins(frequencies, fold):
    order = bin_order(frequencies)[0].reshape(-1, 1, fold)
    return np.broadcast_to(order, (order.shape[0], 2, fold)).reshape(-1)


def butterfly(x_ref, y_ref, start):
    rows, readings = x_ref.shape
    width = readings // radix

    @pl.loop(0, rows // 16)
    def _(r):
        rs = pl.ds(r * 16, 16)
        ys = pl.ds(start + r * 16, 16)
        for b0 in range(0, width, lanes):
            x = [
                x_ref[rs, a * width + b0 : a * width + b0 + lanes].astype(f32)
                for a in range(radix)
            ]
            even = even_parts(x[0], x[half], [x[a] + x[radix - a] for a in range(1, half)])
            odd = odd_parts([x[a] - x[radix - a] for a in range(1, half)])
            left = slice(b0, b0 + lanes)
            right = slice(width + b0, width + b0 + lanes)
            y_ref[0, ys, left] = even[0].astype(bf16)
            y_ref[0, ys, right] = even[half].astype(bf16)
            for q in range(1, half):
                y_ref[q, ys, left] = even[q].astype(bf16)
                y_ref[q, ys, right] = odd[q - 1].astype(bf16)


def spectrum_kernel(blocks, x_ref, table_ref, out_ref, y_ref):
    rows = x_ref.shape[0]
    step = pl.program_id(0)

    @pl.when(step < blocks)
    def _():
        butterfly(x_ref, y_ref, step * rows)

    @pl.when(step >= blocks)
    def _():
        out_ref[...] = lax.dot_general(
            table_ref[0],
            y_ref[step - blocks],
            (((1,), (1,)), ((), ())),
            preferred_element_type=f32,
        ).astype(bf16)


def time_spectrum(waveforms, table):
    channels, readings = waveforms.shape
    block = lanes if channels % lanes == 0 else channels
    blocks = channels // block
    count = table.shape[1]
    group = lambda i: jnp.maximum(i - blocks, 0)
    return pl.pallas_call(
        functools.partial(spectrum_kernel, blocks),
        out_shape=jax.ShapeDtypeStruct((half * count, channels), bf16),
        grid=(blocks + half,),
        in_specs=[
            pl.BlockSpec((block, readings), lambda i: (jnp.minimum(i, blocks - 1), 0)),
            pl.BlockSpec((1,) + table.shape[1:], lambda i: (group(i), 0, 0)),
        ],
        out_specs=pl.BlockSpec((count, channels), lambda i: (group(i), 0)),
        scratch_shapes=[pltpu.VMEM((half, channels, 2 * readings // radix), bf16)],
        compiler_params=pltpu.CompilerParams(vmem_limit_bytes=vmem_limit),
        name="time_spectrum",
    )(waveforms, table)


def series_parts(zr, zs):
    even = even_parts(zr[0], zs[0], zr[1:])
    odd = odd_parts(zs[1:])
    series = [even[0]]
    series += [even[a] + odd[a - 1] for a in range(1, half)]
    series += [even[half]]
    series += [even[a] - odd[a - 1] for a in range(half - 1, 0, -1)]
    return series


def project(b_ref, block, cols, cos, sin):
    taps = cos.shape[0]
    rank = b_ref.shape[0] // taps
    sums = lax.dot_general(
        b_ref[:, cols], block, (((1,), (1,)), ((), ())), preferred_element_type=f32
    )
    first, second = [], []
    for r in range(rank):
        member = sums[r * taps : (r + 1) * taps]
        first.append(jnp.sum(member * cos, axis=0, keepdims=True))
        second.append(jnp.sum(member * sin, axis=0, keepdims=True))
    return jnp.concatenate(first, axis=0), jnp.concatenate(second, axis=0)


def member_series(fold, first, second, table):
    rank, count = first.shape
    ids = lax.broadcasted_iota(jnp.int32, first.shape, 1)
    spectra = first + jnp.where(
        (ids // fold) % 2 == 0,
        -pltpu.roll(second, count - fold, 1),
        pltpu.roll(second, fold, 1),
    )
    high = spectra.astype(bf16)
    low = (spectra - high.astype(f32)).astype(bf16)
    both = jnp.dot(jnp.concatenate([high, low], axis=0), table, preferred_element_type=f32)
    return both[:rank] + both[rank:]


def synthesis(block, table):
    return lax.dot_general(block, table, (((0,), (0,)), ((), ())), preferred_element_type=f32)


def series_group(fold, group, block, b_ref, table, cos, sin, z_ref, c_ref):
    z_ref[group] = synthesis(block, table)
    first, second = project(b_ref, block, slice(None), cos, sin)
    c_ref[group] = member_series(fold, first, second, table)


def series_end(power_ref, out_ref, z_ref, c_ref):
    width = z_ref.shape[2] // 2
    power_ref[...] = jnp.zeros_like(power_ref)

    @pl.loop(0, z_ref.shape[1] // 16)
    def _(r):
        rs = pl.ds(r * 16, 16)
        for b0 in range(0, width, lanes):
            left = slice(b0, b0 + lanes)
            right = slice(width + b0, width + b0 + lanes)
            parts = series_parts(
                [z_ref[g, rs, left] for g in range(half)],
                [z_ref[g, rs, right] for g in range(half)],
            )
            for a, value in enumerate(parts):
                square = value * value
                power_ref[a, :, left] += square[:8] + square[8:]

    parts = series_parts(
        [c_ref[g, :, :width] for g in range(half)],
        [c_ref[g, :, width:] for g in range(half)],
    )
    for a, value in enumerate(parts):
        out_ref[:, a * width : (a + 1) * width] = value


def series_kernel(fold, b_ref, f_ref, t_ref, cos_ref, sin_ref, power_ref, out_ref, z_ref, c_ref):
    group = pl.program_id(0)
    series_group(
        fold, group, f_ref[...], b_ref, t_ref[0], cos_ref[...], sin_ref[...], z_ref, c_ref
    )

    @pl.when(group == half - 1)
    def _():
        series_end(power_ref, out_ref, z_ref, c_ref)


def power_and_series(turned, filtered, table, readings, fold):
    rank, taps, channels = turned.shape
    rows = filtered.shape[0]
    count, width = table.shape[1], table.shape[2] // 2
    bins = row_bins(rows // 2, fold)
    angle = 2.0 * np.pi * (np.arange(taps)[:, None] * bins[None, :] % readings) / readings
    power, series = pl.pallas_call(
        functools.partial(series_kernel, fold),
        out_shape=(
            jax.ShapeDtypeStruct((radix, 8, width), f32),
            jax.ShapeDtypeStruct((rank, readings), f32),
        ),
        grid=(half,),
        in_specs=[
            pl.BlockSpec((rank * taps, channels), lambda i: (0, 0)),
            pl.BlockSpec((count, channels), lambda i: (i, 0)),
            pl.BlockSpec((1,) + table.shape[1:], lambda i: (i, 0, 0)),
            pl.BlockSpec((taps, count), lambda i: (0, i)),
            pl.BlockSpec((taps, count), lambda i: (0, i)),
        ],
        out_specs=(
            pl.BlockSpec((radix, 8, width), lambda i: (0, 0, 0)),
            pl.BlockSpec((rank, readings), lambda i: (0, 0)),
        ),
        scratch_shapes=[
            pltpu.VMEM((half, channels, 2 * width), f32),
            pltpu.VMEM((half, rank, 2 * width), f32),
        ],
        compiler_params=pltpu.CompilerParams(vmem_limit_bytes=vmem_limit),
        name="power_and_series",
    )(
        turned.reshape(rank * taps, channels),
        filtered,
        table,
        jnp.asarray(np.cos(angle), f32),
        jnp.asarray(np.sin(angle), f32),
    )
    return jnp.sum(power, axis=1).reshape(-1), series


def filter_tables(full_count, block_count, parts):
    n2 = lanes
    n1 = full_count // n2
    order = np.arange(n1).reshape(block_count, parts).T.reshape(-1)
    k1, k2, j = np.arange(n1), np.arange(n2), np.arange(n2)
    a1 = 2.0 * np.pi * ((k1[:, None] * order[None, :]) % n1) / n1
    a2 = 2.0 * np.pi * ((j[:, None] * k2[None, :]) % n2) / n2
    at = 2.0 * np.pi * ((k1[:, None] * j[None, :]) % full_count) / full_count
    c1, s1, c2, s2 = np.cos(a1), np.sin(a1), np.cos(a2), np.sin(a2)
    first = np.block([[c1, s1], [-s1, c1]])
    second = np.block([[c2, -s2], [s2, c2]])
    twist = np.stack([np.cos(at), np.sin(at)])
    wave = k1[:, None] + n1 * k2[None, :]
    magnitude = np.minimum(wave, full_count - wave).astype(np.int32)
    return (
        jnp.asarray(first, bf16),
        jnp.asarray(second, bf16),
        jnp.asarray(first.T.copy(), bf16),
        jnp.asarray(second.T.copy(), bf16),
        jnp.asarray(twist, f32),
        jnp.asarray(magnitude),
    )


def filter_chunk(fold, edges, x_ref, w1_ref, w2_ref, v1_ref, v2_ref, tw_ref, mag_ref, o_ref):
    devices = x_ref.shape[0]
    parts = x_ref.shape[2] // lanes
    n1 = mag_ref.shape[0]
    pieces = []
    for ri in range(2):
        for p in range(parts):
            piece = x_ref[:, ri * fold : (ri + 1) * fold, p * lanes : (p + 1) * lanes]
            pieces.append(jnp.swapaxes(piece.astype(f32), 0, 1).astype(bf16))
    stacked = jnp.concatenate(
        [jnp.concatenate([piece[fi] for piece in pieces], axis=0) for fi in range(fold)], axis=1
    )
    waves = jnp.dot(w1_ref[...], stacked, preferred_element_type=f32)
    tc, ts = tw_ref[0], tw_ref[1]
    rows = []
    for fi in range(fold):
        col = slice(fi * lanes, (fi + 1) * lanes)
        re, im = waves[:n1, col], waves[n1:, col]
        rows.append(
            jnp.concatenate([re * tc + im * ts, im * tc - re * ts], axis=1).astype(bf16)
        )
    waves = jnp.dot(jnp.concatenate(rows, axis=0), w2_ref[...], preferred_element_type=f32)
    mag = mag_ref[...]
    rows = []
    for fi in range(fold):
        low, high, _ = edges[fi]
        passing = (mag >= low) & (mag <= high)
        block = waves[fi * n1 : (fi + 1) * n1]
        rows.append(
            jnp.concatenate(
                [
                    jnp.where(passing, block[:, :lanes], 0.0),
                    jnp.where(passing, block[:, lanes:], 0.0),
                ],
                axis=1,
            ).astype(bf16)
        )
    waves = jnp.dot(jnp.concatenate(rows, axis=0), v2_ref[...], preferred_element_type=f32)
    cols = []
    for fi in range(fold):
        block = waves[fi * n1 : (fi + 1) * n1] * edges[fi][2]
        re, im = block[:, :lanes], block[:, lanes:]
        cols.append(
            jnp.concatenate([re * tc - im * ts, im * tc + re * ts], axis=0).astype(bf16)
        )
    out = jnp.dot(v1_ref[...], jnp.concatenate(cols, axis=1), preferred_element_type=f32)
    for ri in range(2):
        for p in range(parts):
            r0 = (ri * parts + p) * devices
            piece = jnp.stack(
                [out[r0 : r0 + devices, fi * lanes : (fi + 1) * lanes] for fi in range(fold)]
            )
            o_ref[:, ri * fold : (ri + 1) * fold, p * lanes : (p + 1) * lanes] = jnp.swapaxes(
                piece, 0, 1
            ).astype(bf16)


def greet(me, devices):
    barrier = pltpu.get_barrier_semaphore()

    @pl.loop(1, devices)
    def _(off):
        pl.semaphore_signal(barrier, inc=1, device_id={"chan": lax.rem(me + off, devices)})

    pl.semaphore_wait(barrier, devices - 1)


def gram_row(b_ref, taps):
    rank = b_ref.shape[0] // taps
    piece = 8 * max(n for n in range(1, 6) if taps % (8 * n) == 0)
    size = rank * piece
    total = jnp.zeros((size, size), f32)
    for j in range(0, taps, piece):
        rows = jnp.concatenate(
            [b_ref[r * taps + j : r * taps + j + piece] for r in range(rank)], axis=0
        )
        total += lax.dot_general(
            rows, rows, (((1,), (1,)), ((), ())), preferred_element_type=f32
        )
    row = lax.broadcasted_iota(jnp.int32, (size, size), 0)
    col = lax.broadcasted_iota(jnp.int32, (size, size), 1)
    total = jnp.where(row % piece == col % piece, total, 0.0)
    left = lax.broadcasted_iota(jnp.int32, (rank, size), 1) // piece
    left = jnp.where(left == lax.broadcasted_iota(jnp.int32, (rank, size), 0), 1.0, 0.0)
    square = rank * rank
    right = lax.broadcasted_iota(jnp.int32, (size, square), 0) // piece
    spread = lax.broadcasted_iota(jnp.int32, (size, square), 1)
    right = jnp.where(right == spread % rank, 1.0, 0.0)
    wide = jnp.dot(
        jnp.dot(left, total, precision=highest, preferred_element_type=f32),
        right,
        precision=highest,
        preferred_element_type=f32,
    )
    keep = lax.broadcasted_iota(jnp.int32, (rank, square), 1) // rank
    keep = keep == lax.broadcasted_iota(jnp.int32, (rank, square), 0)
    return jnp.sum(jnp.where(keep, wide, 0.0), axis=0, keepdims=True)


def inverse(row, rank):
    square = rank * rank
    packed = jnp.broadcast_to(row, (rank, square))
    spread = lax.broadcasted_iota(jnp.int32, packed.shape, 1)
    packed = jnp.where(
        spread // rank == lax.broadcasted_iota(jnp.int32, packed.shape, 0), packed, 0.0
    )
    pick = lax.broadcasted_iota(jnp.int32, (square, rank), 0) % rank
    pick = jnp.where(pick == lax.broadcasted_iota(jnp.int32, pick.shape, 1), 1.0, 0.0)
    gram = jnp.dot(packed, pick, precision=highest)
    ids = lax.broadcasted_iota(jnp.int32, (rank, 1), 0)
    solved = jnp.where(ids == lax.broadcasted_iota(jnp.int32, (rank, rank), 1), 1.0, 0.0)
    for k in range(rank):
        scale = 1.0 / gram[k : k + 1, k : k + 1]
        pivot_g, pivot_s = gram[k : k + 1] * scale, solved[k : k + 1] * scale
        column = gram[:, k : k + 1]
        gram = jnp.where(ids == k, pivot_g, gram - column * pivot_g)
        solved = jnp.where(ids == k, pivot_s, solved - column * pivot_s)
    return solved


def lag_windows(devices, lag_count, taps):
    most = max(d * lag_count % lanes for d in range(devices))
    return -(-(most + lag_count + taps) // lanes)


def channel_pieces(channels):
    tiles = channels // lanes
    sizes = [2] * ((tiles - 1) // 2) + [1] * (tiles - 2 * ((tiles - 1) // 2))
    starts = np.concatenate([[0], np.cumsum(sizes)[:-1]])
    return [(int(s) * lanes, n * lanes) for s, n in zip(starts, sizes)]


def fused_kernel(fold, bounds_ref, wave_ref, table_ref, basis_ref, cosine_ref, sine_ref, *refs):
    tables, (det_ref, coef_ref, *refs) = refs[:6], refs[6:]
    wave_buf, y_ref, t_ref, b_ref, cos_ref, sin_ref, *refs = refs
    x_ref, got_ref, mid_ref, out_ref, z_ref, last_ref, c_ref, proj_ref, *refs = refs
    power_ref, stage_ref, series_ref, row_ref, window_ref, band_ref, *refs = refs
    gram_ref, grams_ref, inv_ref, *refs = refs
    wave_sem, load_sem, sent, came, piece_came, end_sent, end_came = refs
    chunks, devices, rows, channels = x_ref.shape
    per_chunk = half // chunks
    part = devices // per_chunk
    count = t_ref.shape[1]
    width = t_ref.shape[2] // 2
    readings = radix * width
    rank, lag_count = coef_ref.shape
    taps = b_ref.shape[0] // rank
    bins = count // 2
    full_count = devices * channels
    blocks = channels // lanes
    final = chunks - 1
    early = final * per_chunk
    pieces = channel_pieces(channels)
    me = lax.axis_index("chan")
    barrier = pltpu.get_barrier_semaphore()

    def others(body):
        @pl.loop(1, devices)
        def _(off):
            body(lax.rem(me + off, devices))

    def remote(src, dst, send_sem, recv_sem, peer):
        return pltpu.make_async_remote_copy(
            src_ref=src,
            dst_ref=dst,
            send_sem=send_sem,
            recv_sem=recv_sem,
            device_id={"chan": peer},
        )

    def arrivals(ref, recv_sem):
        remote(ref, ref, end_sent.at[0], recv_sem, lax.rem(me + 1, devices)).wait_recv()

    def departures(ref, send_sem):
        remote(ref, ref, send_sem, end_came.at[0], lax.rem(me + 1, devices)).wait_send()

    def load_wave(b, slot):
        return pltpu.make_async_copy(
            wave_ref.at[pl.ds(pl.multiple_of(b * lanes, lanes), lanes)],
            wave_buf.at[slot],
            wave_sem.at[slot],
        )

    def load_table(k):
        groups = pl.ds(k * per_chunk, per_chunk)
        return pltpu.make_async_copy(table_ref.at[groups], t_ref.at[groups], load_sem.at[k])

    loads = [
        pltpu.make_async_copy(src, dst, load_sem.at[chunks + n])
        for n, (src, dst) in enumerate(
            ((basis_ref, b_ref), (cosine_ref, cos_ref), (sine_ref, sin_ref))
        )
    ]

    load_wave(0, 0).start()
    others(lambda peer: pl.semaphore_signal(barrier, inc=1, device_id={"chan": peer}))
    load_table(0).start()
    load_wave(1, 1).start()

    def spectrum(group, block):
        return lax.dot_general(
            t_ref[group], block, (((1,), (1,)), ((), ())), preferred_element_type=f32
        ).astype(bf16)

    @pl.loop(0, blocks)
    def _(b):
        slot = lax.rem(b, 2)
        cs = pl.ds(pl.multiple_of(b * lanes, lanes), lanes)
        load_wave(b, slot).wait()
        butterfly(wave_buf.at[slot], y_ref, b * lanes)

        @pl.when(b + 2 < blocks)
        def _():
            load_wave(b + 2, slot).start()

        @pl.when(b == 0)
        def _():
            load_table(0).wait()
            for k in range(1, chunks):
                load_table(k).start()
            for load in loads:
                load.start()
            pl.semaphore_wait(barrier, devices - 1)

        for n in range(per_chunk):
            x_ref[0, n * part : (n + 1) * part, :, cs] = spectrum(n, y_ref[n, cs]).reshape(
                part, rows, lanes
            )
        others(
            lambda peer: remote(
                x_ref.at[0, peer, :, cs], got_ref.at[0, me, :, cs], sent.at[0, 0], came.at[0, 0], peer
            ).start()
        )

    got_ref[0, me] = x_ref[0, me]

    @pl.loop(1, chunks)
    def _(k):
        load_table(k).wait()
        for n in range(per_chunk):
            group = k * per_chunk + n
            x_ref[k, n * part : (n + 1) * part] = spectrum(group, y_ref[group]).reshape(
                part, rows, channels
            )
        others(
            lambda peer: remote(
                x_ref.at[k, peer], got_ref.at[k, me], sent.at[0, k], came.at[0, k], peer
            ).start()
        )
        got_ref[k, me] = x_ref[k, me]

    for load in loads:
        load.wait()
    gram_ref[...] = gram_row(b_ref, taps)
    others(
        lambda peer: remote(
            gram_ref, grams_ref.at[me], end_sent.at[0], end_came.at[0], peer
        ).start()
    )
    grams_ref[me] = gram_ref[...]

    @pl.loop(0, chunks)
    def _(k):
        arrivals(got_ref.at[k, : devices - 1], came.at[0, k])
        place = (k * devices + me) * fold
        group, inside = place // bins, place % bins
        side = inside // (bins // 2)
        base = radix * (inside % (bins // 2))
        base += jnp.where(
            group == 0, half * side, jnp.where(side == 0, group, radix - group)
        )
        edges = []
        for fi in range(fold):
            f = base + radix * fi
            scale = jnp.where(f == 0, 0.5 / full_count, 1.0 / full_count)
            edges.append((bounds_ref[0, f], bounds_ref[1, f], scale))
        filter_chunk(fold, edges, got_ref.at[k], *tables, mid_ref.at[k])

        @pl.when(k < final)
        def _():
            others(
                lambda peer: remote(
                    mid_ref.at[k, peer], out_ref.at[k, me], sent.at[1, k], came.at[1, k], peer
                ).start()
            )

        @pl.when(k == final)
        def _():
            for n, (start, size) in enumerate(pieces):
                cs = pl.ds(start, size)
                others(
                    lambda peer: remote(
                        mid_ref.at[final, peer, :, cs],
                        out_ref.at[final, me, :, cs],
                        sent.at[1, final],
                        piece_came.at[n],
                        peer,
                    ).start()
                )

        out_ref[k, me] = mid_ref[k, me]

    arrivals(grams_ref.at[: devices - 1], end_came.at[0])
    inv_ref[...] = inverse(jnp.sum(grams_ref[...], axis=0), rank)
    first_lag = me * lag_count
    shift = first_lag % lanes
    row = lax.broadcasted_iota(jnp.int32, band_ref.shape, 0)
    lag = row - lax.broadcasted_iota(jnp.int32, band_ref.shape, 1) - shift
    band_ref[...] = jnp.where((lag >= 0) & (lag < taps), 1.0, 0.0).astype(bf16)
    power_ref[...] = jnp.zeros_like(power_ref)

    @pl.loop(0, final)
    def _(k):
        arrivals(out_ref.at[k, : devices - 1], came.at[1, k])
        for n in range(per_chunk):
            block = out_ref[k, n * part : (n + 1) * part].reshape(count, channels)
            group = k * per_chunk + n
            series_group(
                fold, group, block, b_ref, t_ref[group], cos_ref[group], sin_ref[group], z_ref, c_ref
            )

    def last_block(n, start, size):
        return out_ref[final, n * part : (n + 1) * part, :, start : start + size].reshape(count, size)

    def piece_power(start, size):
        for n in range(per_chunk):
            last_ref[n, :size] = synthesis(last_block(n, start, size), t_ref[early + n])

        @pl.loop(0, size // 16)
        def _(r):
            zs, ls = pl.ds(start + r * 16, 16), pl.ds(r * 16, 16)
            for b0 in range(0, width, lanes):
                left = slice(b0, b0 + lanes)
                right = slice(width + b0, width + b0 + lanes)
                parts = series_parts(
                    *(
                        [z_ref[g, zs, side] for g in range(early)]
                        + [last_ref[n, ls, side] for n in range(per_chunk)]
                        for side in (left, right)
                    )
                )
                for a, value in enumerate(parts):
                    square = value * value
                    power_ref[a, :, left] += square[:8] + square[8:]

    for p, (start, size) in enumerate(pieces):
        arrivals(out_ref.at[final, : devices - 1, :, start : start + size], piece_came.at[p])
        if p < len(pieces) - 1:
            piece_power(start, size)
        if p == len(pieces) - 2:
            for n in range(per_chunk):
                first, second = project(
                    b_ref,
                    last_block(n, 0, start + size),
                    slice(0, start + size),
                    cos_ref[early + n],
                    sin_ref[early + n],
                )
                proj_ref[n, 0], proj_ref[n, 1] = first, second
    start, size = pieces[-1]
    for n in range(per_chunk):
        first, second = project(
            b_ref,
            last_block(n, start, size),
            slice(start, start + size),
            cos_ref[early + n],
            sin_ref[early + n],
        )
        c_ref[early + n] = member_series(
            fold, first + proj_ref[n, 0], second + proj_ref[n, 1], t_ref[early + n]
        )

    series = jnp.concatenate(
        series_parts(
            [c_ref[g, :, :width] for g in range(half)],
            [c_ref[g, :, width:] for g in range(half)],
        ),
        axis=1,
    )
    for d in range(devices):
        begin = d * lag_count // lanes * lanes
        off = d * lag_count - begin
        span = -(-(off + lag_count) // lanes) * lanes
        member = series[:, begin : begin + span]
        if off:
            member = pltpu.roll(member, span - off, 1)
        stage_ref[d] = member[:, :lag_count].astype(bf16)
    others(
        lambda peer: remote(
            stage_ref.at[peer], series_ref.at[me], end_sent.at[1], end_came.at[1], peer
        ).start()
    )
    series_ref[me] = stage_ref[me]

    piece_power(start, size)
    power = jnp.sum(power_ref[...], axis=1)
    tiles = width // lanes
    ahead = window_ref.shape[1]
    for a in range(radix):
        for j in range(tiles):
            value = power[a : a + 1, j * lanes : (j + 1) * lanes]
            row_ref[a * tiles + j] = value
            if a * tiles + j < ahead:
                row_ref[radix * tiles + a * tiles + j] = value
    others(
        lambda peer: remote(
            row_ref.at[pl.ds(peer * lag_count // lanes, ahead)],
            window_ref.at[me],
            end_sent.at[2],
            end_came.at[2],
            peer,
        ).start()
    )
    window_ref[me] = row_ref[pl.ds(first_lag // lanes, ahead)]

    arrivals(series_ref.at[: devices - 1], end_came.at[1])
    correlation = jnp.sum(series_ref[...].astype(f32), axis=0) * (2.0 / readings)
    solved = jnp.dot(inv_ref[...], correlation, precision=highest)
    numerator = jnp.sum(correlation * solved, axis=0, keepdims=True)
    arrivals(window_ref.at[: devices - 1], end_came.at[2])
    window = jnp.sum(window_ref[...], axis=0)
    window = jnp.concatenate([window[n] for n in range(ahead)], axis=1)
    top = window.astype(bf16).astype(f32)
    middle = (window - top).astype(bf16).astype(f32)
    ids = lax.broadcasted_iota(jnp.int32, (16, window.shape[1]), 0)
    window = jnp.where(
        ids == 0,
        top,
        jnp.where(ids == 1, middle, jnp.where(ids == 2, window - top - middle, 0.0)),
    ).astype(bf16)
    energy = jnp.sum(
        jnp.dot(window, band_ref[...], preferred_element_type=f32), axis=0, keepdims=True
    ) * ((2.0 / readings) ** 2)
    level = energy / (full_count * taps) + 1e-06
    det_ref[...] = numerator / (rank * level)
    coef_ref[...] = correlation / jnp.sqrt(level)

    @pl.loop(0, chunks)
    def _(k):
        departures(x_ref.at[k, : devices - 1], sent.at[0, k])
        departures(mid_ref.at[k, : devices - 1], sent.at[1, k])

    departures(grams_ref.at[: devices - 1], end_sent.at[0])
    departures(stage_ref.at[: devices - 1], end_sent.at[1])
    departures(window_ref.at[: devices - 1], end_sent.at[2])


def fused(waveforms, turned, bounds, table, devices, fold):
    channels, readings = waveforms.shape
    rank, taps, _ = turned.shape
    frequencies = bounds.shape[1]
    count, width = table.shape[1], table.shape[2] // 2
    chunks = frequencies // devices // fold
    per_chunk = half // chunks
    lag_count = readings // devices
    bins = row_bins(frequencies, fold)
    angle = 2.0 * np.pi * (np.arange(taps)[:, None] * bins[None, :] % readings) / readings
    angle = angle.reshape(taps, half, count).transpose(1, 0, 2)
    tables = filter_tables(devices * channels, devices, channels // lanes)
    ahead = lag_windows(devices, lag_count, taps)
    pieces = channel_pieces(channels)
    smem = pl.BlockSpec(memory_space=pltpu.SMEM)
    vmem = pl.BlockSpec(memory_space=pltpu.VMEM)
    hbm = pl.BlockSpec(memory_space=pl.ANY)
    exchange = pltpu.VMEM((chunks, devices, 2 * fold, channels), bf16)
    dma = pltpu.SemaphoreType.DMA
    return pl.pallas_call(
        functools.partial(fused_kernel, fold),
        out_shape=(
            jax.ShapeDtypeStruct((1, lag_count), f32),
            jax.ShapeDtypeStruct((rank, lag_count), f32),
        ),
        in_specs=[smem] + [hbm] * 5 + [vmem] * len(tables),
        out_specs=(vmem, vmem),
        scratch_shapes=[
            pltpu.VMEM((2, lanes, readings), bf16),
            pltpu.VMEM((half, channels, 2 * width), bf16),
            pltpu.VMEM(table.shape, bf16),
            pltpu.VMEM((rank * taps, channels), bf16),
            pltpu.VMEM(angle.shape, f32),
            pltpu.VMEM(angle.shape, f32),
            exchange,
            exchange,
            exchange,
            exchange,
            pltpu.VMEM((half - per_chunk, channels, 2 * width), f32),
            pltpu.VMEM((per_chunk, max(size for _, size in pieces), 2 * width), f32),
            pltpu.VMEM((half, rank, 2 * width), f32),
            pltpu.VMEM((per_chunk, 2, rank, count), f32),
            pltpu.VMEM((radix, 8, width), f32),
            pltpu.VMEM((devices, rank, lag_count), bf16),
            pltpu.VMEM((devices, rank, lag_count), bf16),
            pltpu.VMEM((readings // lanes + ahead, 1, lanes), f32),
            pltpu.VMEM((devices, ahead, 1, lanes), f32),
            pltpu.VMEM((ahead * lanes, lag_count), bf16),
            pltpu.VMEM((1, rank * rank), f32),
            pltpu.VMEM((devices, 1, rank * rank), f32),
            pltpu.VMEM((rank, rank), f32),
            dma((2,)),
            dma((chunks + 3,)),
            dma((2, chunks)),
            dma((2, chunks)),
            dma((len(pieces),)),
            dma((3,)),
            dma((3,)),
        ],
        compiler_params=pltpu.CompilerParams(
            vmem_limit_bytes=vmem_limit, collective_id=1, has_side_effects=True
        ),
        name="detect_all",
    )(
        bounds,
        waveforms,
        table,
        turned.reshape(rank * taps, channels),
        jnp.asarray(np.cos(angle), f32),
        jnp.asarray(np.sin(angle), f32),
        *tables,
    )


def filter_plain(gathered, edges, scale, fold):
    devices, rows, channels = gathered.shape
    full_count = devices * channels
    values = gathered.reshape(devices, rows // (2 * fold), 2, fold, channels)
    values = values.transpose(2, 1, 3, 0, 4).reshape(2, rows // 2, devices, channels)
    d, m = np.arange(devices), np.arange(channels)
    ad = 2.0 * np.pi * (d[:, None] * d[None, :] % devices) / devices
    am = 2.0 * np.pi * (m[:, None] * m[None, :] % channels) / channels
    at = 2.0 * np.pi * (d[:, None] * m[None, :]) / full_count
    wave = d[:, None] + devices * m[None, :]
    magnitude = jnp.asarray(np.minimum(wave, full_count - wave), jnp.int32)[None]

    def turn(layout, angle, pair, sign):
        c, s = jnp.asarray(np.cos(angle), f32), jnp.asarray(sign * np.sin(angle), f32)
        ein = functools.partial(jnp.einsum, layout, precision=highest)
        return ein(c, pair[0]) - ein(s, pair[1]), ein(c, pair[1]) + ein(s, pair[0])

    def twist(pair, sign):
        c, s = jnp.asarray(np.cos(at), f32), jnp.asarray(sign * np.sin(at), f32)
        return c * pair[0] - s * pair[1], c * pair[1] + s * pair[0]

    pair = (values[0].astype(f32), values[1].astype(f32))
    pair = twist(turn("kp,fpm->fkm", ad, pair, -1.0), -1.0)
    pair = turn("mn,fkm->fkn", am, pair, -1.0)
    passing = (magnitude >= edges[0][:, None, None]) & (magnitude <= edges[1][:, None, None])
    pair = tuple(jnp.where(passing, part, 0.0) for part in pair)
    pair = twist(turn("mn,fkn->fkm", am, pair, 1.0), 1.0)
    pair = turn("kp,fkm->fpm", ad, pair, 1.0)
    out = (jnp.stack(pair) * scale[0][None, :, None, None]).astype(bf16)
    out = out.reshape(2, rows // (2 * fold), fold, devices, channels).transpose(3, 1, 0, 2, 4)
    return out.reshape(devices, rows, channels)


def final_kernel(
    full_count, taps, readings, series_ref, extra_ref, det_ref, coef_ref, got_ref, more_ref, sent, came
):
    devices, rank, lag_count = series_ref.shape
    square = rank * rank
    span = extra_ref.shape[2] - square
    me = lax.axis_index("chan")
    greet(me, devices)

    def copies(peer, slot):
        pair = ((series_ref, got_ref), (extra_ref, more_ref))
        return [
            pltpu.make_async_remote_copy(
                src_ref=src.at[peer],
                dst_ref=dst.at[slot],
                send_sem=sent.at[n, peer],
                recv_sem=came.at[n, slot],
                device_id={"chan": peer},
            )
            for n, (src, dst) in enumerate(pair)
        ]

    @pl.loop(1, devices)
    def _(off):
        for copy in copies(lax.rem(me + off, devices), me):
            copy.start()

    got_ref[me] = series_ref[me]
    more_ref[me] = extra_ref[me]

    @pl.loop(1, devices)
    def _(off):
        peer = lax.rem(me + off, devices)
        for copy in copies(peer, peer):
            copy.wait()

    correlation = jnp.sum(got_ref[...].astype(f32), axis=0) * (2.0 / readings)
    extra = jnp.sum(more_ref[...], axis=0)
    window = extra[:, :span]
    packed = jnp.broadcast_to(extra[:, span:], (rank, square))
    spread = lax.broadcasted_iota(jnp.int32, packed.shape, 1)
    packed = jnp.where(
        spread // rank == lax.broadcasted_iota(jnp.int32, packed.shape, 0), packed, 0.0
    )
    pick = lax.broadcasted_iota(jnp.int32, (square, rank), 0) % rank
    pick = jnp.where(pick == lax.broadcasted_iota(jnp.int32, pick.shape, 1), 1.0, 0.0)
    gram = jnp.dot(packed, pick, precision=highest)
    row = lax.broadcasted_iota(jnp.int32, (window.shape[1], lag_count), 0)
    lag = row - lax.broadcasted_iota(jnp.int32, row.shape, 1)
    band = jnp.where((lag >= 0) & (lag < taps), 1.0, 0.0)
    energy = jnp.dot(
        jnp.broadcast_to(window, (8, window.shape[1])), band, precision=highest
    )[:1] * (2.0 / readings) ** 2
    level = energy / (full_count * taps) + 1e-06
    solved = correlation
    ids = lax.broadcasted_iota(jnp.int32, (rank, 1), 0)
    for k in range(rank):
        inverse = 1.0 / gram[k : k + 1, k : k + 1]
        pivot_g, pivot_c = gram[k : k + 1] * inverse, solved[k : k + 1] * inverse
        column = gram[:, k : k + 1]
        gram = jnp.where(ids == k, pivot_g, gram - column * pivot_g)
        solved = jnp.where(ids == k, pivot_c, solved - column * pivot_c)
    det_ref[...] = jnp.sum(correlation * solved, axis=0, keepdims=True) / (rank * level)
    coef_ref[...] = correlation / jnp.sqrt(level)


def local(waveforms, basis, bounds):
    devices = lax.axis_size("chan")
    position = lax.axis_index("chan")
    channels, readings = waveforms.shape
    rank, _, taps = basis.shape
    frequencies = bounds.shape[1]
    full_count = channels * devices
    bin_count = frequencies // devices
    fold = math.gcd(16, bin_count)
    lag_count = readings // devices

    table = jnp.asarray(time_table(frequencies, readings, fold), bf16)
    turned = jnp.swapaxes(basis, 1, 2)
    chunks = bin_count // fold
    if (
        channels % lanes == 0
        and channels > lanes
        and readings % (radix * lanes) == 0
        and chunks > 1
        and half % chunks == 0
        and devices % (half // chunks) == 0
    ):
        detection, coefficients = fused(waveforms, turned, bounds, table, devices, fold)
        return (detection[0], coefficients)

    spectrum = time_spectrum(waveforms, table)
    flat = basis.reshape(rank, channels * taps)
    gram = jnp.einsum("ka,ja->kj", flat, flat, preferred_element_type=f32)
    order = bin_order(frequencies)[0].reshape(-1)
    edges = lax.dynamic_slice_in_dim(bounds[:, order], position * bin_count, bin_count, 1)
    scale = jnp.asarray(np.where(order == 0, 0.5, 1.0) / full_count, f32).reshape(1, -1)
    scale = lax.dynamic_slice_in_dim(scale, position * bin_count, bin_count, 1)
    spectrum = spectrum.reshape(devices, 2 * bin_count, channels)
    gathered = lax.all_to_all(spectrum, "chan", split_axis=0, concat_axis=0, tiled=True)
    passed = filter_plain(gathered, edges, scale, fold)
    filtered = lax.all_to_all(passed, "chan", split_axis=0, concat_axis=0, tiled=True)
    filtered = filtered.reshape(2 * frequencies, channels)
    power, series = power_and_series(turned, filtered, table, readings, fold)
    ahead = 1 + -(-taps // lag_count)
    span = -(-(lag_count + taps) // lanes) * lanes
    power = power.reshape(devices, lag_count)
    windows = jnp.concatenate([jnp.roll(power, -n, axis=0) for n in range(ahead)], axis=1)
    windows = jnp.pad(windows[:, : lag_count + taps], ((0, 0), (0, span - lag_count - taps)))
    gram = jnp.broadcast_to(gram.reshape(1, -1), (devices, rank * rank))
    extra = jnp.concatenate([windows, gram], axis=1)[:, None, :]
    series = series.astype(bf16).reshape(rank, devices, lag_count).transpose(1, 0, 2)
    vmem = pl.BlockSpec(memory_space=pltpu.VMEM)
    detection, coefficients = pl.pallas_call(
        functools.partial(final_kernel, full_count, taps, readings),
        out_shape=(
            jax.ShapeDtypeStruct((1, lag_count), f32),
            jax.ShapeDtypeStruct((rank, lag_count), f32),
        ),
        in_specs=[vmem, vmem],
        out_specs=(vmem, vmem),
        scratch_shapes=[
            pltpu.VMEM(series.shape, bf16),
            pltpu.VMEM(extra.shape, f32),
            pltpu.SemaphoreType.DMA((2, devices)),
            pltpu.SemaphoreType.DMA((2, devices)),
        ],
        compiler_params=pltpu.CompilerParams(
            vmem_limit_bytes=vmem_limit, collective_id=0, has_side_effects=True
        ),
        name="detect",
    )(series, extra)
    return (detection[0], coefficients)


def solution(mesh):
    in_specs = (P("chan", "groups"), P(None, "chan", None), P())
    out_specs = (P(("groups", "chan")), P(None, ("groups", "chan")))
    return jax.shard_map(local, mesh=mesh, in_specs=in_specs, out_specs=out_specs, check_vma=False)
```

```python
import functools
import math

import jax
import jax.numpy as jnp
import numpy as np
from jax import lax
from jax.experimental import pallas as pl
from jax.experimental.pallas import tpu as pltpu
from jax.sharding import PartitionSpec as P

radix = 12
half = radix // 2
lanes = 128
highest = lax.Precision.HIGHEST
bf16 = jnp.bfloat16
f32 = jnp.float32
vmem_limit = 60 * 1024 * 1024


def even_parts(x0, x6, s):
    r = math.sqrt(3.0) / 2.0
    s1, s2, s3, s4, s5 = s
    u, v = x0 + x6, x0 - x6
    e24, d24, e15, d15 = s2 + s4, s2 - s4, s1 + s5, s1 - s5
    even0, odd0 = u + e24, e15 + s3
    even1, odd1 = v + 0.5 * d24, r * d15
    even2, odd2 = u - 0.5 * e24, 0.5 * e15 - s3
    return (
        even0 + odd0,
        even1 + odd1,
        even2 + odd2,
        v - d24,
        even2 - odd2,
        even1 - odd1,
        even0 - odd0,
    )


def odd_parts(d):
    r = math.sqrt(3.0) / 2.0
    d1, d2, d3, d4, d5 = d
    e15, m15 = d1 + d5, d1 - d5
    odd1, even1 = 0.5 * e15 + d3, r * (d2 + d4)
    odd2, even2 = r * m15, r * (d2 - d4)
    return (odd1 + even1, odd2 + even2, e15 - d3, odd2 - even2, odd1 - even1)


def bin_order(frequencies):
    ids = np.arange(frequencies)
    groups = [np.concatenate([ids[ids % radix == 0], ids[ids % radix == half]])]
    signs = [np.ones(frequencies // half)]
    for q in range(1, half):
        plus, minus = ids[ids % radix == q], ids[ids % radix == radix - q]
        groups.append(np.concatenate([plus, minus]))
        signs.append(np.concatenate([np.ones(len(plus)), -np.ones(len(minus))]))
    return np.stack(groups), np.stack(signs)


def time_table(frequencies, readings, fold):
    width = readings // radix
    groups, signs = bin_order(frequencies)
    theta = (groups[:, :, None] * np.arange(width)[None, None, :] % readings) * (
        2.0 * np.pi / readings
    )
    cos, sin = np.cos(theta), np.sin(theta)
    sg = signs[:, :, None]
    real = np.concatenate([cos, -sg * sin], axis=2)
    imag = np.concatenate([-sin, -sg * cos], axis=2)
    first = (groups[0] % radix == 0)[:, None]
    real[0] = np.concatenate([np.where(first, cos[0], 0), np.where(first, 0, cos[0])], axis=1)
    imag[0] = np.concatenate([np.where(first, -sin[0], 0), np.where(first, 0, -sin[0])], axis=1)
    count = groups.shape[1]
    both = np.stack([real, imag], axis=1).reshape(half, 2, count // fold, fold, 2 * width)
    return both.transpose(0, 2, 1, 3, 4).reshape(half, 2 * count, 2 * width)


def row_bins(frequencies, fold):
    order = bin_order(frequencies)[0].reshape(-1, 1, fold)
    return np.broadcast_to(order, (order.shape[0], 2, fold)).reshape(-1)


def butterfly(x_ref, y_ref, start):
    rows, readings = x_ref.shape
    width = readings // radix

    @pl.loop(0, rows // 16)
    def _(r):
        rs = pl.ds(r * 16, 16)
        ys = pl.ds(start + r * 16, 16)
        for b0 in range(0, width, lanes):
            x = [
                x_ref[rs, a * width + b0 : a * width + b0 + lanes].astype(f32)
                for a in range(radix)
            ]
            even = even_parts(x[0], x[half], [x[a] + x[radix - a] for a in range(1, half)])
            odd = odd_parts([x[a] - x[radix - a] for a in range(1, half)])
            left = slice(b0, b0 + lanes)
            right = slice(width + b0, width + b0 + lanes)
            y_ref[0, ys, left] = even[0].astype(bf16)
            y_ref[0, ys, right] = even[half].astype(bf16)
            for q in range(1, half):
                y_ref[q, ys, left] = even[q].astype(bf16)
                y_ref[q, ys, right] = odd[q - 1].astype(bf16)


def spectrum_kernel(blocks, x_ref, table_ref, out_ref, y_ref):
    rows = x_ref.shape[0]
    step = pl.program_id(0)

    @pl.when(step < blocks)
    def _():
        butterfly(x_ref, y_ref, step * rows)

    @pl.when(step >= blocks)
    def _():
        out_ref[...] = lax.dot_general(
            table_ref[0],
            y_ref[step - blocks],
            (((1,), (1,)), ((), ())),
            preferred_element_type=f32,
        ).astype(bf16)


def time_spectrum(waveforms, table):
    channels, readings = waveforms.shape
    block = lanes if channels % lanes == 0 else channels
    blocks = channels // block
    count = table.shape[1]
    group = lambda i: jnp.maximum(i - blocks, 0)
    return pl.pallas_call(
        functools.partial(spectrum_kernel, blocks),
        out_shape=jax.ShapeDtypeStruct((half * count, channels), bf16),
        grid=(blocks + half,),
        in_specs=[
            pl.BlockSpec((block, readings), lambda i: (jnp.minimum(i, blocks - 1), 0)),
            pl.BlockSpec((1,) + table.shape[1:], lambda i: (group(i), 0, 0)),
        ],
        out_specs=pl.BlockSpec((count, channels), lambda i: (group(i), 0)),
        scratch_shapes=[pltpu.VMEM((half, channels, 2 * readings // radix), bf16)],
        compiler_params=pltpu.CompilerParams(vmem_limit_bytes=vmem_limit),
        name="time_spectrum",
    )(waveforms, table)


def series_parts(zr, zs):
    even = even_parts(zr[0], zs[0], zr[1:])
    odd = odd_parts(zs[1:])
    series = [even[0]]
    series += [even[a] + odd[a - 1] for a in range(1, half)]
    series += [even[half]]
    series += [even[a] - odd[a - 1] for a in range(half - 1, 0, -1)]
    return series


def project(b_ref, block, cols, cos, sin):
    taps = cos.shape[0]
    rank = b_ref.shape[0] // taps
    sums = lax.dot_general(
        b_ref[:, cols], block, (((1,), (1,)), ((), ())), preferred_element_type=f32
    )
    first, second = [], []
    for r in range(rank):
        member = sums[r * taps : (r + 1) * taps]
        first.append(jnp.sum(member * cos, axis=0, keepdims=True))
        second.append(jnp.sum(member * sin, axis=0, keepdims=True))
    return jnp.concatenate(first, axis=0), jnp.concatenate(second, axis=0)


def member_series(fold, first, second, table):
    rank, count = first.shape
    ids = lax.broadcasted_iota(jnp.int32, first.shape, 1)
    spectra = first + jnp.where(
        (ids // fold) % 2 == 0,
        -pltpu.roll(second, count - fold, 1),
        pltpu.roll(second, fold, 1),
    )
    high = spectra.astype(bf16)
    low = (spectra - high.astype(f32)).astype(bf16)
    both = jnp.dot(jnp.concatenate([high, low], axis=0), table, preferred_element_type=f32)
    return both[:rank] + both[rank:]


def synthesis(block, table):
    return lax.dot_general(block, table, (((0,), (0,)), ((), ())), preferred_element_type=f32)


def series_group(fold, group, block, b_ref, table, cos, sin, z_ref, c_ref):
    z_ref[group] = synthesis(block, table)
    first, second = project(b_ref, block, slice(None), cos, sin)
    c_ref[group] = member_series(fold, first, second, table)


def series_end(power_ref, out_ref, z_ref, c_ref):
    width = z_ref.shape[2] // 2
    power_ref[...] = jnp.zeros_like(power_ref)

    @pl.loop(0, z_ref.shape[1] // 16)
    def _(r):
        rs = pl.ds(r * 16, 16)
        for b0 in range(0, width, lanes):
            left = slice(b0, b0 + lanes)
            right = slice(width + b0, width + b0 + lanes)
            parts = series_parts(
                [z_ref[g, rs, left] for g in range(half)],
                [z_ref[g, rs, right] for g in range(half)],
            )
            for a, value in enumerate(parts):
                square = value * value
                power_ref[a, :, left] += square[:8] + square[8:]

    parts = series_parts(
        [c_ref[g, :, :width] for g in range(half)],
        [c_ref[g, :, width:] for g in range(half)],
    )
    for a, value in enumerate(parts):
        out_ref[:, a * width : (a + 1) * width] = value


def series_kernel(fold, b_ref, f_ref, t_ref, cos_ref, sin_ref, power_ref, out_ref, z_ref, c_ref):
    group = pl.program_id(0)
    series_group(
        fold, group, f_ref[...], b_ref, t_ref[0], cos_ref[...], sin_ref[...], z_ref, c_ref
    )

    @pl.when(group == half - 1)
    def _():
        series_end(power_ref, out_ref, z_ref, c_ref)


def power_and_series(turned, filtered, table, readings, fold):
    rank, taps, channels = turned.shape
    rows = filtered.shape[0]
    count, width = table.shape[1], table.shape[2] // 2
    bins = row_bins(rows // 2, fold)
    angle = 2.0 * np.pi * (np.arange(taps)[:, None] * bins[None, :] % readings) / readings
    power, series = pl.pallas_call(
        functools.partial(series_kernel, fold),
        out_shape=(
            jax.ShapeDtypeStruct((radix, 8, width), f32),
            jax.ShapeDtypeStruct((rank, readings), f32),
        ),
        grid=(half,),
        in_specs=[
            pl.BlockSpec((rank * taps, channels), lambda i: (0, 0)),
            pl.BlockSpec((count, channels), lambda i: (i, 0)),
            pl.BlockSpec((1,) + table.shape[1:], lambda i: (i, 0, 0)),
            pl.BlockSpec((taps, count), lambda i: (0, i)),
            pl.BlockSpec((taps, count), lambda i: (0, i)),
        ],
        out_specs=(
            pl.BlockSpec((radix, 8, width), lambda i: (0, 0, 0)),
            pl.BlockSpec((rank, readings), lambda i: (0, 0)),
        ),
        scratch_shapes=[
            pltpu.VMEM((half, channels, 2 * width), f32),
            pltpu.VMEM((half, rank, 2 * width), f32),
        ],
        compiler_params=pltpu.CompilerParams(vmem_limit_bytes=vmem_limit),
        name="power_and_series",
    )(
        turned.reshape(rank * taps, channels),
        filtered,
        table,
        jnp.asarray(np.cos(angle), f32),
        jnp.asarray(np.sin(angle), f32),
    )
    return jnp.sum(power, axis=1).reshape(-1), series


def filter_tables(full_count, block_count, parts):
    n2 = lanes
    n1 = full_count // n2
    order = np.arange(n1).reshape(block_count, parts).T.reshape(-1)
    k1, k2, j = np.arange(n1), np.arange(n2), np.arange(n2)
    a1 = 2.0 * np.pi * ((k1[:, None] * order[None, :]) % n1) / n1
    a2 = 2.0 * np.pi * ((j[:, None] * k2[None, :]) % n2) / n2
    at = 2.0 * np.pi * ((k1[:, None] * j[None, :]) % full_count) / full_count
    c1, s1, c2, s2 = np.cos(a1), np.sin(a1), np.cos(a2), np.sin(a2)
    first = np.block([[c1, s1], [-s1, c1]])
    second = np.block([[c2, -s2], [s2, c2]])
    twist = np.stack([np.cos(at), np.sin(at)])
    wave = k1[:, None] + n1 * k2[None, :]
    magnitude = np.minimum(wave, full_count - wave).astype(np.int32)
    return (
        jnp.asarray(first, bf16),
        jnp.asarray(second, bf16),
        jnp.asarray(first.T.copy(), bf16),
        jnp.asarray(second.T.copy(), bf16),
        jnp.asarray(twist, f32),
        jnp.asarray(magnitude),
    )


def filter_chunk(fold, edges, x_ref, w1_ref, w2_ref, v1_ref, v2_ref, tw_ref, mag_ref, o_ref):
    devices = x_ref.shape[0]
    parts = x_ref.shape[2] // lanes
    n1 = mag_ref.shape[0]
    pieces = []
    for ri in range(2):
        for p in range(parts):
            piece = x_ref[:, ri * fold : (ri + 1) * fold, p * lanes : (p + 1) * lanes]
            pieces.append(jnp.swapaxes(piece.astype(f32), 0, 1).astype(bf16))
    stacked = jnp.concatenate(
        [jnp.concatenate([piece[fi] for piece in pieces], axis=0) for fi in range(fold)], axis=1
    )
    waves = jnp.dot(w1_ref[...], stacked, preferred_element_type=f32)
    tc, ts = tw_ref[0], tw_ref[1]
    rows = []
    for fi in range(fold):
        col = slice(fi * lanes, (fi + 1) * lanes)
        re, im = waves[:n1, col], waves[n1:, col]
        rows.append(
            jnp.concatenate([re * tc + im * ts, im * tc - re * ts], axis=1).astype(bf16)
        )
    waves = jnp.dot(jnp.concatenate(rows, axis=0), w2_ref[...], preferred_element_type=f32)
    mag = mag_ref[...]
    rows = []
    for fi in range(fold):
        low, high, _ = edges[fi]
        passing = (mag >= low) & (mag <= high)
        block = waves[fi * n1 : (fi + 1) * n1]
        rows.append(
            jnp.concatenate(
                [
                    jnp.where(passing, block[:, :lanes], 0.0),
                    jnp.where(passing, block[:, lanes:], 0.0),
                ],
                axis=1,
            ).astype(bf16)
        )
    waves = jnp.dot(jnp.concatenate(rows, axis=0), v2_ref[...], preferred_element_type=f32)
    cols = []
    for fi in range(fold):
        block = waves[fi * n1 : (fi + 1) * n1] * edges[fi][2]
        re, im = block[:, :lanes], block[:, lanes:]
        cols.append(
            jnp.concatenate([re * tc - im * ts, im * tc + re * ts], axis=0).astype(bf16)
        )
    out = jnp.dot(v1_ref[...], jnp.concatenate(cols, axis=1), preferred_element_type=f32)
    for ri in range(2):
        for p in range(parts):
            r0 = (ri * parts + p) * devices
            piece = jnp.stack(
                [out[r0 : r0 + devices, fi * lanes : (fi + 1) * lanes] for fi in range(fold)]
            )
            o_ref[:, ri * fold : (ri + 1) * fold, p * lanes : (p + 1) * lanes] = jnp.swapaxes(
                piece, 0, 1
            ).astype(bf16)


def greet(me, devices):
    barrier = pltpu.get_barrier_semaphore()

    @pl.loop(1, devices)
    def _(off):
        pl.semaphore_signal(barrier, inc=1, device_id={"chan": lax.rem(me + off, devices)})

    pl.semaphore_wait(barrier, devices - 1)


def gram_row(b_ref, taps):
    rank = b_ref.shape[0] // taps
    piece = 8 * max(n for n in range(1, 6) if taps % (8 * n) == 0)
    size = rank * piece
    total = jnp.zeros((size, size), f32)
    for j in range(0, taps, piece):
        rows = jnp.concatenate(
            [b_ref[r * taps + j : r * taps + j + piece] for r in range(rank)], axis=0
        )
        total += lax.dot_general(
            rows, rows, (((1,), (1,)), ((), ())), preferred_element_type=f32
        )
    row = lax.broadcasted_iota(jnp.int32, (size, size), 0)
    col = lax.broadcasted_iota(jnp.int32, (size, size), 1)
    total = jnp.where(row % piece == col % piece, total, 0.0)
    left = lax.broadcasted_iota(jnp.int32, (rank, size), 1) // piece
    left = jnp.where(left == lax.broadcasted_iota(jnp.int32, (rank, size), 0), 1.0, 0.0)
    square = rank * rank
    right = lax.broadcasted_iota(jnp.int32, (size, square), 0) // piece
    spread = lax.broadcasted_iota(jnp.int32, (size, square), 1)
    right = jnp.where(right == spread % rank, 1.0, 0.0)
    wide = jnp.dot(
        jnp.dot(left, total, precision=highest, preferred_element_type=f32),
        right,
        precision=highest,
        preferred_element_type=f32,
    )
    keep = lax.broadcasted_iota(jnp.int32, (rank, square), 1) // rank
    keep = keep == lax.broadcasted_iota(jnp.int32, (rank, square), 0)
    return jnp.sum(jnp.where(keep, wide, 0.0), axis=0, keepdims=True)


def inverse(row, rank):
    square = rank * rank
    packed = jnp.broadcast_to(row, (rank, square))
    spread = lax.broadcasted_iota(jnp.int32, packed.shape, 1)
    packed = jnp.where(
        spread // rank == lax.broadcasted_iota(jnp.int32, packed.shape, 0), packed, 0.0
    )
    pick = lax.broadcasted_iota(jnp.int32, (square, rank), 0) % rank
    pick = jnp.where(pick == lax.broadcasted_iota(jnp.int32, pick.shape, 1), 1.0, 0.0)
    gram = jnp.dot(packed, pick, precision=highest)
    ids = lax.broadcasted_iota(jnp.int32, (rank, 1), 0)
    solved = jnp.where(ids == lax.broadcasted_iota(jnp.int32, (rank, rank), 1), 1.0, 0.0)
    for k in range(rank):
        scale = 1.0 / gram[k : k + 1, k : k + 1]
        pivot_g, pivot_s = gram[k : k + 1] * scale, solved[k : k + 1] * scale
        column = gram[:, k : k + 1]
        gram = jnp.where(ids == k, pivot_g, gram - column * pivot_g)
        solved = jnp.where(ids == k, pivot_s, solved - column * pivot_s)
    return solved


def lag_windows(devices, lag_count, taps):
    most = max(d * lag_count % lanes for d in range(devices))
    return -(-(most + lag_count + taps) // lanes)


def channel_pieces(channels):
    tiles = channels // lanes
    sizes = [2] * ((tiles - 1) // 2) + [1] * (tiles - 2 * ((tiles - 1) // 2))
    starts = np.concatenate([[0], np.cumsum(sizes)[:-1]])
    return [(int(s) * lanes, n * lanes) for s, n in zip(starts, sizes)]


def fused_kernel(fold, bounds_ref, wave_ref, table_ref, *refs):
    late, (det_ref, coef_ref, *refs) = refs[:9], refs[9:]
    tables, refs = refs[:6], refs[6:]
    wave_buf, y_ref, t_ref, b_ref, cos_ref, sin_ref, *refs = refs
    x_ref, got_ref, mid_ref, out_ref, z_ref, last_ref, c_ref, proj_ref, *refs = refs
    power_ref, stage_ref, series_ref, row_ref, window_ref, band_ref, *refs = refs
    gram_ref, grams_ref, inv_ref, *refs = refs
    wave_sem, load_sem, sent, came, piece_came, end_sent, end_came = refs
    chunks, devices, rows, channels = x_ref.shape
    per_chunk = half // chunks
    part = devices // per_chunk
    count = t_ref.shape[1]
    width = t_ref.shape[2] // 2
    readings = radix * width
    rank, lag_count = coef_ref.shape
    taps = b_ref.shape[0] // rank
    bins = count // 2
    full_count = devices * channels
    blocks = channels // lanes
    final = chunks - 1
    early = final * per_chunk
    pieces = channel_pieces(channels)
    me = lax.axis_index("chan")
    barrier = pltpu.get_barrier_semaphore()

    def others(body):
        @pl.loop(1, devices)
        def _(off):
            body(lax.rem(me + off, devices))

    def remote(src, dst, send_sem, recv_sem, peer):
        return pltpu.make_async_remote_copy(
            src_ref=src,
            dst_ref=dst,
            send_sem=send_sem,
            recv_sem=recv_sem,
            device_id={"chan": peer},
        )

    def arrivals(ref, recv_sem):
        remote(ref, ref, end_sent.at[0], recv_sem, lax.rem(me + 1, devices)).wait_recv()

    def departures(ref, send_sem):
        remote(ref, ref, send_sem, end_came.at[0], lax.rem(me + 1, devices)).wait_send()

    def load_wave(b, slot):
        return pltpu.make_async_copy(
            wave_ref.at[pl.ds(pl.multiple_of(b * lanes, lanes), lanes)],
            wave_buf.at[slot],
            wave_sem.at[slot],
        )

    def load_table(k):
        groups = pl.ds(k * per_chunk, per_chunk)
        return pltpu.make_async_copy(table_ref.at[groups], t_ref.at[groups], load_sem.at[k])

    loads = [
        pltpu.make_async_copy(src, dst, load_sem.at[chunks + n])
        for n, (src, dst) in enumerate(zip(late, (*tables, b_ref, cos_ref, sin_ref)))
    ]

    load_wave(0, 0).start()
    others(lambda peer: pl.semaphore_signal(barrier, inc=1, device_id={"chan": peer}))
    load_table(0).start()
    load_wave(1, 1).start()

    def spectrum(group, block):
        return lax.dot_general(
            t_ref[group], block, (((1,), (1,)), ((), ())), preferred_element_type=f32
        ).astype(bf16)

    @pl.loop(0, blocks)
    def _(b):
        slot = lax.rem(b, 2)
        cs = pl.ds(pl.multiple_of(b * lanes, lanes), lanes)
        load_wave(b, slot).wait()
        butterfly(wave_buf.at[slot], y_ref, b * lanes)

        @pl.when(b + 2 < blocks)
        def _():
            load_wave(b + 2, slot).start()

        @pl.when(b == blocks - 2)
        def _():
            for k in range(1, chunks):
                load_table(k).start()
            for load in loads:
                load.start()

        @pl.when(b == 0)
        def _():
            load_table(0).wait()
            pl.semaphore_wait(barrier, devices - 1)

        for n in range(per_chunk):
            x_ref[0, n * part : (n + 1) * part, :, cs] = spectrum(n, y_ref[n, cs]).reshape(
                part, rows, lanes
            )
        others(
            lambda peer: remote(
                x_ref.at[0, peer, :, cs], got_ref.at[0, me, :, cs], sent.at[0, 0], came.at[0, 0], peer
            ).start()
        )

    got_ref[0, me] = x_ref[0, me]

    @pl.loop(1, chunks)
    def _(k):
        load_table(k).wait()
        for n in range(per_chunk):
            group = k * per_chunk + n
            x_ref[k, n * part : (n + 1) * part] = spectrum(group, y_ref[group]).reshape(
                part, rows, channels
            )
        others(
            lambda peer: remote(
                x_ref.at[k, peer], got_ref.at[k, me], sent.at[0, k], came.at[0, k], peer
            ).start()
        )
        got_ref[k, me] = x_ref[k, me]

    for load in loads:
        load.wait()
    gram_ref[...] = gram_row(b_ref, taps)
    others(
        lambda peer: remote(
            gram_ref, grams_ref.at[me], end_sent.at[0], end_came.at[0], peer
        ).start()
    )
    grams_ref[me] = gram_ref[...]

    @pl.loop(0, chunks)
    def _(k):
        arrivals(got_ref.at[k, : devices - 1], came.at[0, k])
        place = (k * devices + me) * fold
        group, inside = place // bins, place % bins
        side = inside // (bins // 2)
        base = radix * (inside % (bins // 2))
        base += jnp.where(
            group == 0, half * side, jnp.where(side == 0, group, radix - group)
        )
        edges = []
        for fi in range(fold):
            f = base + radix * fi
            scale = jnp.where(f == 0, 0.5 / full_count, 1.0 / full_count)
            edges.append((bounds_ref[0, f], bounds_ref[1, f], scale))
        filter_chunk(fold, edges, got_ref.at[k], *tables, mid_ref.at[k])

        @pl.when(k < final)
        def _():
            others(
                lambda peer: remote(
                    mid_ref.at[k, peer], out_ref.at[k, me], sent.at[1, k], came.at[1, k], peer
                ).start()
            )

        @pl.when(k == final)
        def _():
            for n, (start, size) in enumerate(pieces):
                cs = pl.ds(start, size)
                others(
                    lambda peer: remote(
                        mid_ref.at[final, peer, :, cs],
                        out_ref.at[final, me, :, cs],
                        sent.at[1, final],
                        piece_came.at[n],
                        peer,
                    ).start()
                )

        out_ref[k, me] = mid_ref[k, me]

    arrivals(grams_ref.at[: devices - 1], end_came.at[0])
    inv_ref[...] = inverse(jnp.sum(grams_ref[...], axis=0), rank)
    first_lag = me * lag_count
    shift = first_lag % lanes
    row = lax.broadcasted_iota(jnp.int32, band_ref.shape, 0)
    lag = row - lax.broadcasted_iota(jnp.int32, band_ref.shape, 1) - shift
    band_ref[...] = jnp.where((lag >= 0) & (lag < taps), 1.0, 0.0).astype(bf16)
    power_ref[...] = jnp.zeros_like(power_ref)

    @pl.loop(0, final)
    def _(k):
        arrivals(out_ref.at[k, : devices - 1], came.at[1, k])
        for n in range(per_chunk):
            block = out_ref[k, n * part : (n + 1) * part].reshape(count, channels)
            group = k * per_chunk + n
            series_group(
                fold, group, block, b_ref, t_ref[group], cos_ref[group], sin_ref[group], z_ref, c_ref
            )

    def last_block(n, start, size):
        return out_ref[final, n * part : (n + 1) * part, :, start : start + size].reshape(count, size)

    def piece_power(start, size):
        for n in range(per_chunk):
            last_ref[n, :size] = synthesis(last_block(n, start, size), t_ref[early + n])

        @pl.loop(0, size // 16)
        def _(r):
            zs, ls = pl.ds(start + r * 16, 16), pl.ds(r * 16, 16)
            for b0 in range(0, width, lanes):
                left = slice(b0, b0 + lanes)
                right = slice(width + b0, width + b0 + lanes)
                parts = series_parts(
                    *(
                        [z_ref[g, zs, side] for g in range(early)]
                        + [last_ref[n, ls, side] for n in range(per_chunk)]
                        for side in (left, right)
                    )
                )
                for a, value in enumerate(parts):
                    square = value * value
                    power_ref[a, :, left] += square[:8] + square[8:]

    def piece_project(start, size):
        for n in range(per_chunk):
            both = project(
                b_ref,
                last_block(n, start, size),
                slice(start, start + size),
                cos_ref[early + n],
                sin_ref[early + n],
            )
            for i, value in enumerate(both):
                proj_ref[n, i] = value if start == 0 else proj_ref[n, i] + value

    shown = len(pieces) - 2
    for p, (start, size) in enumerate(pieces):
        arrivals(out_ref.at[final, : devices - 1, :, start : start + size], piece_came.at[p])
        piece_project(start, size)
        if p < shown:
            piece_power(start, size)
    for n in range(per_chunk):
        c_ref[early + n] = member_series(fold, proj_ref[n, 0], proj_ref[n, 1], t_ref[early + n])

    series = jnp.concatenate(
        series_parts(
            [c_ref[g, :, :width] for g in range(half)],
            [c_ref[g, :, width:] for g in range(half)],
        ),
        axis=1,
    )
    for d in range(devices):
        begin = d * lag_count // lanes * lanes
        off = d * lag_count - begin
        span = -(-(off + lag_count) // lanes) * lanes
        member = series[:, begin : begin + span]
        if off:
            member = pltpu.roll(member, span - off, 1)
        stage_ref[d] = member[:, :lag_count].astype(bf16)
    others(
        lambda peer: remote(
            stage_ref.at[peer], series_ref.at[me], end_sent.at[1], end_came.at[1], peer
        ).start()
    )
    series_ref[me] = stage_ref[me]

    for start, size in pieces[max(shown, 0) :]:
        piece_power(start, size)
    power = jnp.sum(power_ref[...], axis=1)
    tiles = width // lanes
    ahead = window_ref.shape[1]
    for a in range(radix):
        for j in range(tiles):
            value = power[a : a + 1, j * lanes : (j + 1) * lanes]
            row_ref[a * tiles + j] = value
            if a * tiles + j < ahead:
                row_ref[radix * tiles + a * tiles + j] = value
    others(
        lambda peer: remote(
            row_ref.at[pl.ds(peer * lag_count // lanes, ahead)],
            window_ref.at[me],
            end_sent.at[2],
            end_came.at[2],
            peer,
        ).start()
    )
    window_ref[me] = row_ref[pl.ds(first_lag // lanes, ahead)]

    arrivals(series_ref.at[: devices - 1], end_came.at[1])
    correlation = jnp.sum(series_ref[...].astype(f32), axis=0) * (2.0 / readings)
    solved = jnp.dot(inv_ref[...], correlation, precision=highest)
    numerator = jnp.sum(correlation * solved, axis=0, keepdims=True)
    arrivals(window_ref.at[: devices - 1], end_came.at[2])
    window = jnp.sum(window_ref[...], axis=0)
    window = jnp.concatenate([window[n] for n in range(ahead)], axis=1)
    top = window.astype(bf16).astype(f32)
    middle = (window - top).astype(bf16).astype(f32)
    ids = lax.broadcasted_iota(jnp.int32, (16, window.shape[1]), 0)
    window = jnp.where(
        ids == 0,
        top,
        jnp.where(ids == 1, middle, jnp.where(ids == 2, window - top - middle, 0.0)),
    ).astype(bf16)
    energy = jnp.sum(
        jnp.dot(window, band_ref[...], preferred_element_type=f32), axis=0, keepdims=True
    ) * ((2.0 / readings) ** 2)
    level = energy / (full_count * taps) + 1e-06
    det_ref[...] = numerator / (rank * level)
    coef_ref[...] = correlation / jnp.sqrt(level)

    @pl.loop(0, chunks)
    def _(k):
        departures(x_ref.at[k, : devices - 1], sent.at[0, k])
        departures(mid_ref.at[k, : devices - 1], sent.at[1, k])

    departures(grams_ref.at[: devices - 1], end_sent.at[0])
    departures(stage_ref.at[: devices - 1], end_sent.at[1])
    departures(window_ref.at[: devices - 1], end_sent.at[2])


def fused(waveforms, turned, bounds, table, devices, fold):
    channels, readings = waveforms.shape
    rank, taps, _ = turned.shape
    frequencies = bounds.shape[1]
    count, width = table.shape[1], table.shape[2] // 2
    chunks = frequencies // devices // fold
    per_chunk = half // chunks
    lag_count = readings // devices
    bins = row_bins(frequencies, fold)
    angle = 2.0 * np.pi * (np.arange(taps)[:, None] * bins[None, :] % readings) / readings
    angle = angle.reshape(taps, half, count).transpose(1, 0, 2)
    tables = filter_tables(devices * channels, devices, channels // lanes)
    ahead = lag_windows(devices, lag_count, taps)
    pieces = channel_pieces(channels)
    smem = pl.BlockSpec(memory_space=pltpu.SMEM)
    vmem = pl.BlockSpec(memory_space=pltpu.VMEM)
    hbm = pl.BlockSpec(memory_space=pl.ANY)
    exchange = pltpu.VMEM((chunks, devices, 2 * fold, channels), bf16)
    dma = pltpu.SemaphoreType.DMA
    return pl.pallas_call(
        functools.partial(fused_kernel, fold),
        out_shape=(
            pltpu.VMEM((1, lag_count), f32),
            pltpu.VMEM((rank, lag_count), f32),
        ),
        in_specs=[smem] + [hbm] * (5 + len(tables)),
        out_specs=(vmem, vmem),
        scratch_shapes=[
            *(pltpu.VMEM(t.shape, t.dtype) for t in tables),
            pltpu.VMEM((2, lanes, readings), bf16),
            pltpu.VMEM((half, channels, 2 * width), bf16),
            pltpu.VMEM(table.shape, bf16),
            pltpu.VMEM((rank * taps, channels), bf16),
            pltpu.VMEM(angle.shape, f32),
            pltpu.VMEM(angle.shape, f32),
            exchange,
            exchange,
            exchange,
            exchange,
            pltpu.VMEM((half - per_chunk, channels, 2 * width), f32),
            pltpu.VMEM((per_chunk, max(size for _, size in pieces), 2 * width), f32),
            pltpu.VMEM((half, rank, 2 * width), f32),
            pltpu.VMEM((per_chunk, 2, rank, count), f32),
            pltpu.VMEM((radix, 8, width), f32),
            pltpu.VMEM((devices, rank, lag_count), bf16),
            pltpu.VMEM((devices, rank, lag_count), bf16),
            pltpu.VMEM((readings // lanes + ahead, 1, lanes), f32),
            pltpu.VMEM((devices, ahead, 1, lanes), f32),
            pltpu.VMEM((ahead * lanes, lag_count), bf16),
            pltpu.VMEM((1, rank * rank), f32),
            pltpu.VMEM((devices, 1, rank * rank), f32),
            pltpu.VMEM((rank, rank), f32),
            dma((2,)),
            dma((chunks + 3 + len(tables),)),
            dma((2, chunks)),
            dma((2, chunks)),
            dma((len(pieces),)),
            dma((3,)),
            dma((3,)),
        ],
        compiler_params=pltpu.CompilerParams(
            vmem_limit_bytes=vmem_limit, collective_id=1, has_side_effects=True
        ),
        name="detect_all",
    )(
        bounds,
        waveforms,
        table,
        *tables,
        turned.reshape(rank * taps, channels),
        jnp.asarray(np.cos(angle), f32),
        jnp.asarray(np.sin(angle), f32),
    )


def filter_plain(gathered, edges, scale, fold):
    devices, rows, channels = gathered.shape
    full_count = devices * channels
    values = gathered.reshape(devices, rows // (2 * fold), 2, fold, channels)
    values = values.transpose(2, 1, 3, 0, 4).reshape(2, rows // 2, devices, channels)
    d, m = np.arange(devices), np.arange(channels)
    ad = 2.0 * np.pi * (d[:, None] * d[None, :] % devices) / devices
    am = 2.0 * np.pi * (m[:, None] * m[None, :] % channels) / channels
    at = 2.0 * np.pi * (d[:, None] * m[None, :]) / full_count
    wave = d[:, None] + devices * m[None, :]
    magnitude = jnp.asarray(np.minimum(wave, full_count - wave), jnp.int32)[None]

    def turn(layout, angle, pair, sign):
        c, s = jnp.asarray(np.cos(angle), f32), jnp.asarray(sign * np.sin(angle), f32)
        ein = functools.partial(jnp.einsum, layout, precision=highest)
        return ein(c, pair[0]) - ein(s, pair[1]), ein(c, pair[1]) + ein(s, pair[0])

    def twist(pair, sign):
        c, s = jnp.asarray(np.cos(at), f32), jnp.asarray(sign * np.sin(at), f32)
        return c * pair[0] - s * pair[1], c * pair[1] + s * pair[0]

    pair = (values[0].astype(f32), values[1].astype(f32))
    pair = twist(turn("kp,fpm->fkm", ad, pair, -1.0), -1.0)
    pair = turn("mn,fkm->fkn", am, pair, -1.0)
    passing = (magnitude >= edges[0][:, None, None]) & (magnitude <= edges[1][:, None, None])
    pair = tuple(jnp.where(passing, part, 0.0) for part in pair)
    pair = twist(turn("mn,fkn->fkm", am, pair, 1.0), 1.0)
    pair = turn("kp,fkm->fpm", ad, pair, 1.0)
    out = (jnp.stack(pair) * scale[0][None, :, None, None]).astype(bf16)
    out = out.reshape(2, rows // (2 * fold), fold, devices, channels).transpose(3, 1, 0, 2, 4)
    return out.reshape(devices, rows, channels)


def final_kernel(
    full_count, taps, readings, series_ref, extra_ref, det_ref, coef_ref, got_ref, more_ref, sent, came
):
    devices, rank, lag_count = series_ref.shape
    square = rank * rank
    span = extra_ref.shape[2] - square
    me = lax.axis_index("chan")
    greet(me, devices)

    def copies(peer, slot):
        pair = ((series_ref, got_ref), (extra_ref, more_ref))
        return [
            pltpu.make_async_remote_copy(
                src_ref=src.at[peer],
                dst_ref=dst.at[slot],
                send_sem=sent.at[n, peer],
                recv_sem=came.at[n, slot],
                device_id={"chan": peer},
            )
            for n, (src, dst) in enumerate(pair)
        ]

    @pl.loop(1, devices)
    def _(off):
        for copy in copies(lax.rem(me + off, devices), me):
            copy.start()

    got_ref[me] = series_ref[me]
    more_ref[me] = extra_ref[me]

    @pl.loop(1, devices)
    def _(off):
        peer = lax.rem(me + off, devices)
        for copy in copies(peer, peer):
            copy.wait()

    correlation = jnp.sum(got_ref[...].astype(f32), axis=0) * (2.0 / readings)
    extra = jnp.sum(more_ref[...], axis=0)
    window = extra[:, :span]
    packed = jnp.broadcast_to(extra[:, span:], (rank, square))
    spread = lax.broadcasted_iota(jnp.int32, packed.shape, 1)
    packed = jnp.where(
        spread // rank == lax.broadcasted_iota(jnp.int32, packed.shape, 0), packed, 0.0
    )
    pick = lax.broadcasted_iota(jnp.int32, (square, rank), 0) % rank
    pick = jnp.where(pick == lax.broadcasted_iota(jnp.int32, pick.shape, 1), 1.0, 0.0)
    gram = jnp.dot(packed, pick, precision=highest)
    row = lax.broadcasted_iota(jnp.int32, (window.shape[1], lag_count), 0)
    lag = row - lax.broadcasted_iota(jnp.int32, row.shape, 1)
    band = jnp.where((lag >= 0) & (lag < taps), 1.0, 0.0)
    energy = jnp.dot(
        jnp.broadcast_to(window, (8, window.shape[1])), band, precision=highest
    )[:1] * (2.0 / readings) ** 2
    level = energy / (full_count * taps) + 1e-06
    solved = correlation
    ids = lax.broadcasted_iota(jnp.int32, (rank, 1), 0)
    for k in range(rank):
        inverse = 1.0 / gram[k : k + 1, k : k + 1]
        pivot_g, pivot_c = gram[k : k + 1] * inverse, solved[k : k + 1] * inverse
        column = gram[:, k : k + 1]
        gram = jnp.where(ids == k, pivot_g, gram - column * pivot_g)
        solved = jnp.where(ids == k, pivot_c, solved - column * pivot_c)
    det_ref[...] = jnp.sum(correlation * solved, axis=0, keepdims=True) / (rank * level)
    coef_ref[...] = correlation / jnp.sqrt(level)


def local(waveforms, basis, bounds):
    devices = lax.axis_size("chan")
    position = lax.axis_index("chan")
    channels, readings = waveforms.shape
    rank, _, taps = basis.shape
    frequencies = bounds.shape[1]
    full_count = channels * devices
    bin_count = frequencies // devices
    fold = math.gcd(8, bin_count)
    lag_count = readings // devices

    table = jnp.asarray(time_table(frequencies, readings, fold), bf16)
    turned = jnp.swapaxes(basis, 1, 2)
    chunks = bin_count // fold
    if (
        channels % lanes == 0
        and channels > lanes
        and readings % (radix * lanes) == 0
        and chunks > 1
        and half % chunks == 0
        and devices % (half // chunks) == 0
    ):
        detection, coefficients = fused(waveforms, turned, bounds, table, devices, fold)
        return (detection[0], coefficients)

    spectrum = time_spectrum(waveforms, table)
    flat = basis.reshape(rank, channels * taps)
    gram = jnp.einsum("ka,ja->kj", flat, flat, preferred_element_type=f32)
    order = bin_order(frequencies)[0].reshape(-1)
    edges = lax.dynamic_slice_in_dim(bounds[:, order], position * bin_count, bin_count, 1)
    scale = jnp.asarray(np.where(order == 0, 0.5, 1.0) / full_count, f32).reshape(1, -1)
    scale = lax.dynamic_slice_in_dim(scale, position * bin_count, bin_count, 1)
    spectrum = spectrum.reshape(devices, 2 * bin_count, channels)
    gathered = lax.all_to_all(spectrum, "chan", split_axis=0, concat_axis=0, tiled=True)
    passed = filter_plain(gathered, edges, scale, fold)
    filtered = lax.all_to_all(passed, "chan", split_axis=0, concat_axis=0, tiled=True)
    filtered = filtered.reshape(2 * frequencies, channels)
    power, series = power_and_series(turned, filtered, table, readings, fold)
    ahead = 1 + -(-taps // lag_count)
    span = -(-(lag_count + taps) // lanes) * lanes
    power = power.reshape(devices, lag_count)
    windows = jnp.concatenate([jnp.roll(power, -n, axis=0) for n in range(ahead)], axis=1)
    windows = jnp.pad(windows[:, : lag_count + taps], ((0, 0), (0, span - lag_count - taps)))
    gram = jnp.broadcast_to(gram.reshape(1, -1), (devices, rank * rank))
    extra = jnp.concatenate([windows, gram], axis=1)[:, None, :]
    series = series.astype(bf16).reshape(rank, devices, lag_count).transpose(1, 0, 2)
    vmem = pl.BlockSpec(memory_space=pltpu.VMEM)
    detection, coefficients = pl.pallas_call(
        functools.partial(final_kernel, full_count, taps, readings),
        out_shape=(
            jax.ShapeDtypeStruct((1, lag_count), f32),
            jax.ShapeDtypeStruct((rank, lag_count), f32),
        ),
        in_specs=[vmem, vmem],
        out_specs=(vmem, vmem),
        scratch_shapes=[
            pltpu.VMEM(series.shape, bf16),
            pltpu.VMEM(extra.shape, f32),
            pltpu.SemaphoreType.DMA((2, devices)),
            pltpu.SemaphoreType.DMA((2, devices)),
        ],
        compiler_params=pltpu.CompilerParams(
            vmem_limit_bytes=vmem_limit, collective_id=0, has_side_effects=True
        ),
        name="detect",
    )(series, extra)
    return (detection[0], coefficients)


def solution(mesh):
    in_specs = (P("chan", "groups"), P(None, "chan", None), P())
    out_specs = (P(("groups", "chan")), P(None, ("groups", "chan")))
    return jax.shard_map(local, mesh=mesh, in_specs=in_specs, out_specs=out_specs, check_vma=False)
```

```python
import functools
import math

import jax
import jax.numpy as jnp
import numpy as np
from jax import lax
from jax.experimental import pallas as pl
from jax.experimental.pallas import tpu as pltpu
from jax.sharding import PartitionSpec as P

radix = 12
half = radix // 2
lanes = 128
highest = lax.Precision.HIGHEST
bf16 = jnp.bfloat16
f32 = jnp.float32
vmem_limit = 60 * 1024 * 1024


def even_parts(x0, x6, s):
    r = math.sqrt(3.0) / 2.0
    s1, s2, s3, s4, s5 = s
    u, v = x0 + x6, x0 - x6
    e24, d24, e15, d15 = s2 + s4, s2 - s4, s1 + s5, s1 - s5
    even0, odd0 = u + e24, e15 + s3
    even1, odd1 = v + 0.5 * d24, r * d15
    even2, odd2 = u - 0.5 * e24, 0.5 * e15 - s3
    return (
        even0 + odd0,
        even1 + odd1,
        even2 + odd2,
        v - d24,
        even2 - odd2,
        even1 - odd1,
        even0 - odd0,
    )


def odd_parts(d):
    r = math.sqrt(3.0) / 2.0
    d1, d2, d3, d4, d5 = d
    e15, m15 = d1 + d5, d1 - d5
    odd1, even1 = 0.5 * e15 + d3, r * (d2 + d4)
    odd2, even2 = r * m15, r * (d2 - d4)
    return (odd1 + even1, odd2 + even2, e15 - d3, odd2 - even2, odd1 - even1)


def bin_order(frequencies):
    ids = np.arange(frequencies)
    groups = [np.concatenate([ids[ids % radix == 0], ids[ids % radix == half]])]
    signs = [np.ones(frequencies // half)]
    for q in range(1, half):
        plus, minus = ids[ids % radix == q], ids[ids % radix == radix - q]
        groups.append(np.concatenate([plus, minus]))
        signs.append(np.concatenate([np.ones(len(plus)), -np.ones(len(minus))]))
    return np.stack(groups), np.stack(signs)


def time_table(frequencies, readings, fold):
    width = readings // radix
    groups, signs = bin_order(frequencies)
    theta = (groups[:, :, None] * np.arange(width)[None, None, :] % readings) * (
        2.0 * np.pi / readings
    )
    cos, sin = np.cos(theta), np.sin(theta)
    sg = signs[:, :, None]
    real = np.concatenate([cos, -sg * sin], axis=2)
    imag = np.concatenate([-sin, -sg * cos], axis=2)
    first = (groups[0] % radix == 0)[:, None]
    real[0] = np.concatenate([np.where(first, cos[0], 0), np.where(first, 0, cos[0])], axis=1)
    imag[0] = np.concatenate([np.where(first, -sin[0], 0), np.where(first, 0, -sin[0])], axis=1)
    count = groups.shape[1]
    both = np.stack([real, imag], axis=1).reshape(half, 2, count // fold, fold, 2 * width)
    return both.transpose(0, 2, 1, 3, 4).reshape(half, 2 * count, 2 * width)


def row_bins(frequencies, fold):
    order = bin_order(frequencies)[0].reshape(-1, 1, fold)
    return np.broadcast_to(order, (order.shape[0], 2, fold)).reshape(-1)


def butterfly(x_ref, y_ref, start):
    rows, readings = x_ref.shape
    width = readings // radix

    @pl.loop(0, rows // 16)
    def _(r):
        rs = pl.ds(r * 16, 16)
        ys = pl.ds(start + r * 16, 16)
        for b0 in range(0, width, lanes):
            x = [
                x_ref[rs, a * width + b0 : a * width + b0 + lanes].astype(f32)
                for a in range(radix)
            ]
            even = even_parts(x[0], x[half], [x[a] + x[radix - a] for a in range(1, half)])
            odd = odd_parts([x[a] - x[radix - a] for a in range(1, half)])
            left = slice(b0, b0 + lanes)
            right = slice(width + b0, width + b0 + lanes)
            y_ref[0, ys, left] = even[0].astype(bf16)
            y_ref[0, ys, right] = even[half].astype(bf16)
            for q in range(1, half):
                y_ref[q, ys, left] = even[q].astype(bf16)
                y_ref[q, ys, right] = odd[q - 1].astype(bf16)


def spectrum_kernel(blocks, x_ref, table_ref, out_ref, y_ref):
    rows = x_ref.shape[0]
    step = pl.program_id(0)

    @pl.when(step < blocks)
    def _():
        butterfly(x_ref, y_ref, step * rows)

    @pl.when(step >= blocks)
    def _():
        out_ref[...] = lax.dot_general(
            table_ref[0],
            y_ref[step - blocks],
            (((1,), (1,)), ((), ())),
            preferred_element_type=f32,
        ).astype(bf16)


def time_spectrum(waveforms, table):
    channels, readings = waveforms.shape
    block = lanes if channels % lanes == 0 else channels
    blocks = channels // block
    count = table.shape[1]
    group = lambda i: jnp.maximum(i - blocks, 0)
    return pl.pallas_call(
        functools.partial(spectrum_kernel, blocks),
        out_shape=jax.ShapeDtypeStruct((half * count, channels), bf16),
        grid=(blocks + half,),
        in_specs=[
            pl.BlockSpec((block, readings), lambda i: (jnp.minimum(i, blocks - 1), 0)),
            pl.BlockSpec((1,) + table.shape[1:], lambda i: (group(i), 0, 0)),
        ],
        out_specs=pl.BlockSpec((count, channels), lambda i: (group(i), 0)),
        scratch_shapes=[pltpu.VMEM((half, channels, 2 * readings // radix), bf16)],
        compiler_params=pltpu.CompilerParams(vmem_limit_bytes=vmem_limit),
        name="time_spectrum",
    )(waveforms, table)


def series_parts(zr, zs):
    even = even_parts(zr[0], zs[0], zr[1:])
    odd = odd_parts(zs[1:])
    series = [even[0]]
    series += [even[a] + odd[a - 1] for a in range(1, half)]
    series += [even[half]]
    series += [even[a] - odd[a - 1] for a in range(half - 1, 0, -1)]
    return series


def project(b_ref, block, cos, sin):
    taps = cos.shape[0]
    rank = b_ref.shape[0] // taps
    step = math.gcd(4, rank)
    first, second = [], []
    for r0 in range(0, rank, step):
        sums = lax.dot_general(
            b_ref[r0 * taps : (r0 + step) * taps],
            block,
            (((1,), (1,)), ((), ())),
            preferred_element_type=f32,
        )
        for r in range(step):
            member = sums[r * taps : (r + 1) * taps]
            first.append(jnp.sum(member * cos, axis=0, keepdims=True))
            second.append(jnp.sum(member * sin, axis=0, keepdims=True))
    return jnp.concatenate(first, axis=0), jnp.concatenate(second, axis=0)


def member_series(fold, first, second, table):
    rank, count = first.shape
    ids = lax.broadcasted_iota(jnp.int32, first.shape, 1)
    spectra = first + jnp.where(
        (ids // fold) % 2 == 0,
        -pltpu.roll(second, count - fold, 1),
        pltpu.roll(second, fold, 1),
    )
    high = spectra.astype(bf16)
    low = (spectra - high.astype(f32)).astype(bf16)
    both = jnp.dot(jnp.concatenate([high, low], axis=0), table, preferred_element_type=f32)
    return both[:rank] + both[rank:]


def synthesis(block, table):
    return lax.dot_general(block, table, (((0,), (0,)), ((), ())), preferred_element_type=f32)


def series_group(fold, group, block, b_ref, table, cos, sin, z_ref, c_ref):
    z_ref[group] = synthesis(block, table)
    first, second = project(b_ref, block, cos, sin)
    c_ref[group] = member_series(fold, first, second, table)


def sum_power(power_ref, z_ref):
    width = z_ref.shape[2] // 2
    power_ref[...] = jnp.zeros_like(power_ref)

    @pl.loop(0, z_ref.shape[1] // 16)
    def _(r):
        rs = pl.ds(r * 16, 16)
        for b0 in range(0, width, lanes):
            left = slice(b0, b0 + lanes)
            right = slice(width + b0, width + b0 + lanes)
            parts = series_parts(
                [z_ref[g, rs, left] for g in range(half)],
                [z_ref[g, rs, right] for g in range(half)],
            )
            for a, value in enumerate(parts):
                square = value * value
                power_ref[a, :, left] += square[:8] + square[8:]


def series_end(power_ref, out_ref, z_ref, c_ref):
    width = z_ref.shape[2] // 2
    sum_power(power_ref, z_ref)
    parts = series_parts(
        [c_ref[g, :, :width] for g in range(half)],
        [c_ref[g, :, width:] for g in range(half)],
    )
    for a, value in enumerate(parts):
        out_ref[:, a * width : (a + 1) * width] = value


def series_kernel(fold, b_ref, f_ref, t_ref, cos_ref, sin_ref, power_ref, out_ref, z_ref, c_ref):
    group = pl.program_id(0)
    series_group(
        fold, group, f_ref[...], b_ref, t_ref[0], cos_ref[...], sin_ref[...], z_ref, c_ref
    )

    @pl.when(group == half - 1)
    def _():
        series_end(power_ref, out_ref, z_ref, c_ref)


def power_and_series(turned, filtered, table, readings, fold):
    rank, taps, channels = turned.shape
    rows = filtered.shape[0]
    count, width = table.shape[1], table.shape[2] // 2
    bins = row_bins(rows // 2, fold)
    angle = 2.0 * np.pi * (np.arange(taps)[:, None] * bins[None, :] % readings) / readings
    power, series = pl.pallas_call(
        functools.partial(series_kernel, fold),
        out_shape=(
            jax.ShapeDtypeStruct((radix, 8, width), f32),
            jax.ShapeDtypeStruct((rank, readings), f32),
        ),
        grid=(half,),
        in_specs=[
            pl.BlockSpec((rank * taps, channels), lambda i: (0, 0)),
            pl.BlockSpec((count, channels), lambda i: (i, 0)),
            pl.BlockSpec((1,) + table.shape[1:], lambda i: (i, 0, 0)),
            pl.BlockSpec((taps, count), lambda i: (0, i)),
            pl.BlockSpec((taps, count), lambda i: (0, i)),
        ],
        out_specs=(
            pl.BlockSpec((radix, 8, width), lambda i: (0, 0, 0)),
            pl.BlockSpec((rank, readings), lambda i: (0, 0)),
        ),
        scratch_shapes=[
            pltpu.VMEM((half, channels, 2 * width), f32),
            pltpu.VMEM((half, rank, 2 * width), f32),
        ],
        compiler_params=pltpu.CompilerParams(vmem_limit_bytes=vmem_limit),
        name="power_and_series",
    )(
        turned.reshape(rank * taps, channels),
        filtered,
        table,
        jnp.asarray(np.cos(angle), f32),
        jnp.asarray(np.sin(angle), f32),
    )
    return jnp.sum(power, axis=1).reshape(-1), series


def filter_tables(full_count, block_count, parts):
    n2 = lanes
    n1 = full_count // n2
    order = np.arange(n1).reshape(block_count, parts).T.reshape(-1)
    k1, k2, j = np.arange(n1), np.arange(n2), np.arange(n2)
    a1 = 2.0 * np.pi * ((k1[:, None] * order[None, :]) % n1) / n1
    a2 = 2.0 * np.pi * ((j[:, None] * k2[None, :]) % n2) / n2
    at = 2.0 * np.pi * ((k1[:, None] * j[None, :]) % full_count) / full_count
    c1, s1, c2, s2 = np.cos(a1), np.sin(a1), np.cos(a2), np.sin(a2)
    first = np.block([[c1, s1], [-s1, c1]])
    second = np.block([[c2, -s2], [s2, c2]])
    twist = np.stack([np.cos(at), np.sin(at)])
    wave = k1[:, None] + n1 * k2[None, :]
    magnitude = np.minimum(wave, full_count - wave).astype(np.int32)
    return (
        jnp.asarray(first, bf16),
        jnp.asarray(second, bf16),
        jnp.asarray(first.T.copy(), bf16),
        jnp.asarray(second.T.copy(), bf16),
        jnp.asarray(twist, f32),
        jnp.asarray(magnitude),
    )


def filter_chunk(fold, edges, x_ref, w1_ref, w2_ref, v1_ref, v2_ref, tw_ref, mag_ref, o_ref):
    devices = x_ref.shape[0]
    parts = x_ref.shape[2] // lanes
    n1 = mag_ref.shape[0]
    pieces = []
    for ri in range(2):
        for p in range(parts):
            piece = x_ref[:, ri * fold : (ri + 1) * fold, p * lanes : (p + 1) * lanes]
            pieces.append(jnp.swapaxes(piece.astype(f32), 0, 1).astype(bf16))
    stacked = jnp.concatenate(
        [jnp.concatenate([piece[fi] for piece in pieces], axis=0) for fi in range(fold)], axis=1
    )
    waves = jnp.dot(w1_ref[...], stacked, preferred_element_type=f32)
    tc, ts = tw_ref[0], tw_ref[1]
    rows = []
    for fi in range(fold):
        col = slice(fi * lanes, (fi + 1) * lanes)
        re, im = waves[:n1, col], waves[n1:, col]
        rows.append(
            jnp.concatenate([re * tc + im * ts, im * tc - re * ts], axis=1).astype(bf16)
        )
    waves = jnp.dot(jnp.concatenate(rows, axis=0), w2_ref[...], preferred_element_type=f32)
    mag = mag_ref[...]
    rows = []
    for fi in range(fold):
        low, high, _ = edges[fi]
        passing = (mag >= low) & (mag <= high)
        block = waves[fi * n1 : (fi + 1) * n1]
        rows.append(
            jnp.concatenate(
                [
                    jnp.where(passing, block[:, :lanes], 0.0),
                    jnp.where(passing, block[:, lanes:], 0.0),
                ],
                axis=1,
            ).astype(bf16)
        )
    waves = jnp.dot(jnp.concatenate(rows, axis=0), v2_ref[...], preferred_element_type=f32)
    cols = []
    for fi in range(fold):
        block = waves[fi * n1 : (fi + 1) * n1] * edges[fi][2]
        re, im = block[:, :lanes], block[:, lanes:]
        cols.append(
            jnp.concatenate([re * tc - im * ts, im * tc + re * ts], axis=0).astype(bf16)
        )
    out = jnp.dot(v1_ref[...], jnp.concatenate(cols, axis=1), preferred_element_type=f32)
    for ri in range(2):
        for p in range(parts):
            r0 = (ri * parts + p) * devices
            piece = jnp.stack(
                [out[r0 : r0 + devices, fi * lanes : (fi + 1) * lanes] for fi in range(fold)]
            )
            o_ref[:, ri * fold : (ri + 1) * fold, p * lanes : (p + 1) * lanes] = jnp.swapaxes(
                piece, 0, 1
            ).astype(bf16)


def greet(me, devices):
    barrier = pltpu.get_barrier_semaphore()

    @pl.loop(1, devices)
    def _(off):
        pl.semaphore_signal(barrier, inc=1, device_id={"chan": lax.rem(me + off, devices)})

    pl.semaphore_wait(barrier, devices - 1)


def gram_row(b_ref, taps):
    rank = b_ref.shape[0] // taps
    piece = 8 * max(n for n in range(1, 6) if taps % (8 * n) == 0)
    size = rank * piece
    total = jnp.zeros((size, size), f32)
    for j in range(0, taps, piece):
        rows = jnp.concatenate(
            [b_ref[r * taps + j : r * taps + j + piece] for r in range(rank)], axis=0
        )
        total += lax.dot_general(
            rows, rows, (((1,), (1,)), ((), ())), preferred_element_type=f32
        )
    row = lax.broadcasted_iota(jnp.int32, (size, size), 0)
    col = lax.broadcasted_iota(jnp.int32, (size, size), 1)
    total = jnp.where(row % piece == col % piece, total, 0.0)
    left = lax.broadcasted_iota(jnp.int32, (rank, size), 1) // piece
    left = jnp.where(left == lax.broadcasted_iota(jnp.int32, (rank, size), 0), 1.0, 0.0)
    square = rank * rank
    right = lax.broadcasted_iota(jnp.int32, (size, square), 0) // piece
    spread = lax.broadcasted_iota(jnp.int32, (size, square), 1)
    right = jnp.where(right == spread % rank, 1.0, 0.0)
    wide = jnp.dot(
        jnp.dot(left, total, precision=highest, preferred_element_type=f32),
        right,
        precision=highest,
        preferred_element_type=f32,
    )
    keep = lax.broadcasted_iota(jnp.int32, (rank, square), 1) // rank
    keep = keep == lax.broadcasted_iota(jnp.int32, (rank, square), 0)
    return jnp.sum(jnp.where(keep, wide, 0.0), axis=0, keepdims=True)


def inverse(row, rank):
    square = rank * rank
    packed = jnp.broadcast_to(row, (rank, square))
    spread = lax.broadcasted_iota(jnp.int32, packed.shape, 1)
    packed = jnp.where(
        spread // rank == lax.broadcasted_iota(jnp.int32, packed.shape, 0), packed, 0.0
    )
    pick = lax.broadcasted_iota(jnp.int32, (square, rank), 0) % rank
    pick = jnp.where(pick == lax.broadcasted_iota(jnp.int32, pick.shape, 1), 1.0, 0.0)
    gram = jnp.dot(packed, pick, precision=highest)
    ids = lax.broadcasted_iota(jnp.int32, (rank, 1), 0)
    solved = jnp.where(ids == lax.broadcasted_iota(jnp.int32, (rank, rank), 1), 1.0, 0.0)
    for k in range(rank):
        scale = 1.0 / gram[k : k + 1, k : k + 1]
        pivot_g, pivot_s = gram[k : k + 1] * scale, solved[k : k + 1] * scale
        column = gram[:, k : k + 1]
        gram = jnp.where(ids == k, pivot_g, gram - column * pivot_g)
        solved = jnp.where(ids == k, pivot_s, solved - column * pivot_s)
    return solved


def lag_windows(devices, lag_count, taps):
    most = max(d * lag_count % lanes for d in range(devices))
    return -(-(most + lag_count + taps) // lanes)


def fused_kernel(fold, bounds_ref, wave_ref, table_ref, *refs):
    late, (det_ref, coef_ref, *refs) = refs[:9], refs[9:]
    tables, refs = refs[:6], refs[6:]
    wave_buf, y_ref, t_ref, b_ref, cos_ref, sin_ref, *refs = refs
    x_ref, got_ref, mid_ref, out_ref, z_ref, c_ref, *refs = refs
    power_ref, stage_ref, series_ref, row_ref, window_ref, band_ref, *refs = refs
    gram_ref, grams_ref, inv_ref, *refs = refs
    wave_sem, load_sem, sent, came, end_sent, end_came = refs
    chunks, devices, rows, channels = x_ref.shape
    per_chunk = half // chunks
    part = devices // per_chunk
    count = t_ref.shape[1]
    width = t_ref.shape[2] // 2
    readings = radix * width
    rank, lag_count = coef_ref.shape
    taps = b_ref.shape[0] // rank
    bins = count // 2
    full_count = devices * channels
    blocks = channels // lanes
    final = chunks - 1
    early = final * per_chunk
    me = lax.axis_index("chan")
    barrier = pltpu.get_barrier_semaphore()

    def others(body):
        @pl.loop(1, devices)
        def _(off):
            body(lax.rem(me + devices - off, devices))

    def remote(src, dst, send_sem, recv_sem, peer):
        return pltpu.make_async_remote_copy(
            src_ref=src,
            dst_ref=dst,
            send_sem=send_sem,
            recv_sem=recv_sem,
            device_id={"chan": peer},
        )

    def arrivals(ref, recv_sem):
        remote(ref, ref, end_sent.at[0], recv_sem, lax.rem(me + 1, devices)).wait_recv()

    def departures(ref, send_sem):
        remote(ref, ref, send_sem, end_came.at[0], lax.rem(me + 1, devices)).wait_send()

    def load_wave(b, slot):
        return pltpu.make_async_copy(
            wave_ref.at[pl.ds(pl.multiple_of(b * lanes, lanes), lanes)],
            wave_buf.at[slot],
            wave_sem.at[slot],
        )

    def load_table(k):
        groups = pl.ds(k * per_chunk, per_chunk)
        return pltpu.make_async_copy(table_ref.at[groups], t_ref.at[groups], load_sem.at[k])

    loads = [
        pltpu.make_async_copy(src, dst, load_sem.at[chunks + n])
        for n, (src, dst) in enumerate(zip(late, (*tables, b_ref, cos_ref, sin_ref)))
    ]

    load_wave(0, 0).start()
    others(lambda peer: pl.semaphore_signal(barrier, inc=1, device_id={"chan": peer}))
    load_table(0).start()
    load_wave(1, 1).start()

    def spectrum(group, block):
        return lax.dot_general(
            t_ref[group], block, (((1,), (1,)), ((), ())), preferred_element_type=f32
        ).astype(bf16)

    @pl.loop(0, blocks)
    def _(b):
        slot = lax.rem(b, 2)
        cs = pl.ds(pl.multiple_of(b * lanes, lanes), lanes)
        load_wave(b, slot).wait()
        butterfly(wave_buf.at[slot], y_ref, b * lanes)

        @pl.when(b + 2 < blocks)
        def _():
            load_wave(b + 2, slot).start()

        @pl.when(b == blocks - 2)
        def _():
            for k in range(1, chunks):
                load_table(k).start()
            for load in loads:
                load.start()

        @pl.when(b == 0)
        def _():
            load_table(0).wait()
            pl.semaphore_wait(barrier, devices - 1)

        for n in range(per_chunk):
            x_ref[0, n * part : (n + 1) * part, :, cs] = spectrum(n, y_ref[n, cs]).reshape(
                part, rows, lanes
            )
        others(
            lambda peer: remote(
                x_ref.at[0, peer, :, cs], got_ref.at[0, me, :, cs], sent.at[0, 0], came.at[0, 0], peer
            ).start()
        )

    got_ref[0, me] = x_ref[0, me]

    @pl.loop(1, chunks)
    def _(k):
        load_table(k).wait()
        for n in range(per_chunk):
            group = k * per_chunk + n
            x_ref[k, n * part : (n + 1) * part] = spectrum(group, y_ref[group]).reshape(
                part, rows, channels
            )
        others(
            lambda peer: remote(
                x_ref.at[k, peer], got_ref.at[k, me], sent.at[0, k], came.at[0, k], peer
            ).start()
        )
        got_ref[k, me] = x_ref[k, me]

    for load in loads:
        load.wait()
    gram_ref[...] = gram_row(b_ref, taps)
    others(
        lambda peer: remote(
            gram_ref, grams_ref.at[me], end_sent.at[0], end_came.at[0], peer
        ).start()
    )
    grams_ref[me] = gram_ref[...]

    @pl.loop(0, chunks)
    def _(k):
        arrivals(got_ref.at[k, : devices - 1], came.at[0, k])
        place = (k * devices + me) * fold
        group, inside = place // bins, place % bins
        side = inside // (bins // 2)
        base = radix * (inside % (bins // 2))
        base += jnp.where(
            group == 0, half * side, jnp.where(side == 0, group, radix - group)
        )
        edges = []
        for fi in range(fold):
            f = base + radix * fi
            scale = jnp.where(f == 0, 0.5 / full_count, 1.0 / full_count)
            edges.append((bounds_ref[0, f], bounds_ref[1, f], scale))
        filter_chunk(fold, edges, got_ref.at[k], *tables, mid_ref.at[k])

        others(
            lambda peer: remote(
                mid_ref.at[k, peer], out_ref.at[k, me], sent.at[1, k], came.at[1, k], peer
            ).start()
        )
        out_ref[k, me] = mid_ref[k, me]

    arrivals(grams_ref.at[: devices - 1], end_came.at[0])
    inv_ref[...] = inverse(jnp.sum(grams_ref[...], axis=0), rank)
    first_lag = me * lag_count
    shift = first_lag % lanes
    row = lax.broadcasted_iota(jnp.int32, band_ref.shape, 0)
    lag = row - lax.broadcasted_iota(jnp.int32, band_ref.shape, 1) - shift
    band_ref[...] = jnp.where((lag >= 0) & (lag < taps), 1.0, 0.0).astype(bf16)

    def returned(k, n):
        return out_ref[k, n * part : (n + 1) * part].reshape(count, channels)

    def member_group(k, n):
        group = k * per_chunk + n
        first, second = project(b_ref, returned(k, n), cos_ref[group], sin_ref[group])
        c_ref[group] = member_series(fold, first, second, t_ref[group])

    @pl.loop(0, final)
    def _(k):
        arrivals(out_ref.at[k, : devices - 1], came.at[1, k])
        for n in range(per_chunk):
            group = k * per_chunk + n
            z_ref[group] = synthesis(returned(k, n), t_ref[group])
            member_group(k, n)

    arrivals(out_ref.at[final, : devices - 1], came.at[1, final])
    for n in range(per_chunk):
        member_group(final, n)

    series = jnp.concatenate(
        series_parts(
            [c_ref[g, :, :width] for g in range(half)],
            [c_ref[g, :, width:] for g in range(half)],
        ),
        axis=1,
    )
    for d in range(devices):
        begin = d * lag_count // lanes * lanes
        off = d * lag_count - begin
        span = -(-(off + lag_count) // lanes) * lanes
        member = series[:, begin : begin + span]
        if off:
            member = pltpu.roll(member, span - off, 1)
        stage_ref[d] = member[:, :lag_count].astype(bf16)
    others(
        lambda peer: remote(
            stage_ref.at[peer], series_ref.at[me], end_sent.at[1], end_came.at[1], peer
        ).start()
    )
    series_ref[me] = stage_ref[me]

    for n in range(per_chunk):
        z_ref[early + n] = synthesis(returned(final, n), t_ref[early + n])
    sum_power(power_ref, z_ref)
    power = jnp.sum(power_ref[...], axis=1)
    tiles = width // lanes
    ahead = window_ref.shape[1]
    for a in range(radix):
        for j in range(tiles):
            value = power[a : a + 1, j * lanes : (j + 1) * lanes]
            row_ref[a * tiles + j] = value
            if a * tiles + j < ahead:
                row_ref[radix * tiles + a * tiles + j] = value
    others(
        lambda peer: remote(
            row_ref.at[pl.ds(peer * lag_count // lanes, ahead)],
            window_ref.at[me],
            end_sent.at[2],
            end_came.at[2],
            peer,
        ).start()
    )
    window_ref[me] = row_ref[pl.ds(first_lag // lanes, ahead)]

    arrivals(series_ref.at[: devices - 1], end_came.at[1])
    correlation = jnp.sum(series_ref[...].astype(f32), axis=0) * (2.0 / readings)
    solved = jnp.dot(inv_ref[...], correlation, precision=highest)
    numerator = jnp.sum(correlation * solved, axis=0, keepdims=True)
    arrivals(window_ref.at[: devices - 1], end_came.at[2])
    window = jnp.sum(window_ref[...], axis=0)
    window = jnp.concatenate([window[n] for n in range(ahead)], axis=1)
    top = window.astype(bf16).astype(f32)
    middle = (window - top).astype(bf16).astype(f32)
    ids = lax.broadcasted_iota(jnp.int32, (16, window.shape[1]), 0)
    window = jnp.where(
        ids == 0,
        top,
        jnp.where(ids == 1, middle, jnp.where(ids == 2, window - top - middle, 0.0)),
    ).astype(bf16)
    energy = jnp.sum(
        jnp.dot(window, band_ref[...], preferred_element_type=f32), axis=0, keepdims=True
    ) * ((2.0 / readings) ** 2)
    level = energy / (full_count * taps) + 1e-06
    det_ref[...] = numerator / (rank * level)
    coef_ref[...] = correlation / jnp.sqrt(level)

    @pl.loop(0, chunks)
    def _(k):
        departures(x_ref.at[k, : devices - 1], sent.at[0, k])
        departures(mid_ref.at[k, : devices - 1], sent.at[1, k])

    departures(grams_ref.at[: devices - 1], end_sent.at[0])
    departures(stage_ref.at[: devices - 1], end_sent.at[1])
    departures(window_ref.at[: devices - 1], end_sent.at[2])


def fused(waveforms, turned, bounds, table, devices, fold):
    channels, readings = waveforms.shape
    rank, taps, _ = turned.shape
    frequencies = bounds.shape[1]
    count, width = table.shape[1], table.shape[2] // 2
    chunks = frequencies // devices // fold
    per_chunk = half // chunks
    lag_count = readings // devices
    bins = row_bins(frequencies, fold)
    angle = 2.0 * np.pi * (np.arange(taps)[:, None] * bins[None, :] % readings) / readings
    angle = angle.reshape(taps, half, count).transpose(1, 0, 2)
    tables = filter_tables(devices * channels, devices, channels // lanes)
    ahead = lag_windows(devices, lag_count, taps)
    smem = pl.BlockSpec(memory_space=pltpu.SMEM)
    vmem = pl.BlockSpec(memory_space=pltpu.VMEM)
    hbm = pl.BlockSpec(memory_space=pl.ANY)
    exchange = pltpu.VMEM((chunks, devices, 2 * fold, channels), bf16)
    dma = pltpu.SemaphoreType.DMA
    return pl.pallas_call(
        functools.partial(fused_kernel, fold),
        out_shape=(
            pltpu.VMEM((1, lag_count), f32),
            pltpu.VMEM((rank, lag_count), f32),
        ),
        in_specs=[smem] + [hbm] * (5 + len(tables)),
        out_specs=(vmem, vmem),
        scratch_shapes=[
            *(pltpu.VMEM(t.shape, t.dtype) for t in tables),
            pltpu.VMEM((2, lanes, readings), bf16),
            pltpu.VMEM((half, channels, 2 * width), bf16),
            pltpu.VMEM(table.shape, bf16),
            pltpu.VMEM((rank * taps, channels), bf16),
            pltpu.VMEM(angle.shape, f32),
            pltpu.VMEM(angle.shape, f32),
            exchange,
            exchange,
            exchange,
            exchange,
            pltpu.VMEM((half, channels, 2 * width), f32),
            pltpu.VMEM((half, rank, 2 * width), f32),
            pltpu.VMEM((radix, 8, width), f32),
            pltpu.VMEM((devices, rank, lag_count), bf16),
            pltpu.VMEM((devices, rank, lag_count), bf16),
            pltpu.VMEM((readings // lanes + ahead, 1, lanes), f32),
            pltpu.VMEM((devices, ahead, 1, lanes), f32),
            pltpu.VMEM((ahead * lanes, lag_count), bf16),
            pltpu.VMEM((1, rank * rank), f32),
            pltpu.VMEM((devices, 1, rank * rank), f32),
            pltpu.VMEM((rank, rank), f32),
            dma((2,)),
            dma((chunks + 3 + len(tables),)),
            dma((2, chunks)),
            dma((2, chunks)),
            dma((3,)),
            dma((3,)),
        ],
        compiler_params=pltpu.CompilerParams(
            vmem_limit_bytes=vmem_limit, collective_id=1, has_side_effects=True
        ),
        name="detect_all",
    )(
        bounds,
        waveforms,
        table,
        *tables,
        turned.reshape(rank * taps, channels),
        jnp.asarray(np.cos(angle), f32),
        jnp.asarray(np.sin(angle), f32),
    )


def filter_plain(gathered, edges, scale, fold):
    devices, rows, channels = gathered.shape
    full_count = devices * channels
    values = gathered.reshape(devices, rows // (2 * fold), 2, fold, channels)
    values = values.transpose(2, 1, 3, 0, 4).reshape(2, rows // 2, devices, channels)
    d, m = np.arange(devices), np.arange(channels)
    ad = 2.0 * np.pi * (d[:, None] * d[None, :] % devices) / devices
    am = 2.0 * np.pi * (m[:, None] * m[None, :] % channels) / channels
    at = 2.0 * np.pi * (d[:, None] * m[None, :]) / full_count
    wave = d[:, None] + devices * m[None, :]
    magnitude = jnp.asarray(np.minimum(wave, full_count - wave), jnp.int32)[None]

    def turn(layout, angle, pair, sign):
        c, s = jnp.asarray(np.cos(angle), f32), jnp.asarray(sign * np.sin(angle), f32)
        ein = functools.partial(jnp.einsum, layout, precision=highest)
        return ein(c, pair[0]) - ein(s, pair[1]), ein(c, pair[1]) + ein(s, pair[0])

    def twist(pair, sign):
        c, s = jnp.asarray(np.cos(at), f32), jnp.asarray(sign * np.sin(at), f32)
        return c * pair[0] - s * pair[1], c * pair[1] + s * pair[0]

    pair = (values[0].astype(f32), values[1].astype(f32))
    pair = twist(turn("kp,fpm->fkm", ad, pair, -1.0), -1.0)
    pair = turn("mn,fkm->fkn", am, pair, -1.0)
    passing = (magnitude >= edges[0][:, None, None]) & (magnitude <= edges[1][:, None, None])
    pair = tuple(jnp.where(passing, part, 0.0) for part in pair)
    pair = twist(turn("mn,fkn->fkm", am, pair, 1.0), 1.0)
    pair = turn("kp,fkm->fpm", ad, pair, 1.0)
    out = (jnp.stack(pair) * scale[0][None, :, None, None]).astype(bf16)
    out = out.reshape(2, rows // (2 * fold), fold, devices, channels).transpose(3, 1, 0, 2, 4)
    return out.reshape(devices, rows, channels)


def final_kernel(
    full_count, taps, readings, series_ref, extra_ref, det_ref, coef_ref, got_ref, more_ref, sent, came
):
    devices, rank, lag_count = series_ref.shape
    square = rank * rank
    span = extra_ref.shape[2] - square
    me = lax.axis_index("chan")
    greet(me, devices)

    def copies(peer, slot):
        pair = ((series_ref, got_ref), (extra_ref, more_ref))
        return [
            pltpu.make_async_remote_copy(
                src_ref=src.at[peer],
                dst_ref=dst.at[slot],
                send_sem=sent.at[n, peer],
                recv_sem=came.at[n, slot],
                device_id={"chan": peer},
            )
            for n, (src, dst) in enumerate(pair)
        ]

    @pl.loop(1, devices)
    def _(off):
        for copy in copies(lax.rem(me + off, devices), me):
            copy.start()

    got_ref[me] = series_ref[me]
    more_ref[me] = extra_ref[me]

    @pl.loop(1, devices)
    def _(off):
        peer = lax.rem(me + off, devices)
        for copy in copies(peer, peer):
            copy.wait()

    correlation = jnp.sum(got_ref[...].astype(f32), axis=0) * (2.0 / readings)
    extra = jnp.sum(more_ref[...], axis=0)
    window = extra[:, :span]
    packed = jnp.broadcast_to(extra[:, span:], (rank, square))
    spread = lax.broadcasted_iota(jnp.int32, packed.shape, 1)
    packed = jnp.where(
        spread // rank == lax.broadcasted_iota(jnp.int32, packed.shape, 0), packed, 0.0
    )
    pick = lax.broadcasted_iota(jnp.int32, (square, rank), 0) % rank
    pick = jnp.where(pick == lax.broadcasted_iota(jnp.int32, pick.shape, 1), 1.0, 0.0)
    gram = jnp.dot(packed, pick, precision=highest)
    row = lax.broadcasted_iota(jnp.int32, (window.shape[1], lag_count), 0)
    lag = row - lax.broadcasted_iota(jnp.int32, row.shape, 1)
    band = jnp.where((lag >= 0) & (lag < taps), 1.0, 0.0)
    energy = jnp.dot(
        jnp.broadcast_to(window, (8, window.shape[1])), band, precision=highest
    )[:1] * (2.0 / readings) ** 2
    level = energy / (full_count * taps) + 1e-06
    solved = correlation
    ids = lax.broadcasted_iota(jnp.int32, (rank, 1), 0)
    for k in range(rank):
        inverse = 1.0 / gram[k : k + 1, k : k + 1]
        pivot_g, pivot_c = gram[k : k + 1] * inverse, solved[k : k + 1] * inverse
        column = gram[:, k : k + 1]
        gram = jnp.where(ids == k, pivot_g, gram - column * pivot_g)
        solved = jnp.where(ids == k, pivot_c, solved - column * pivot_c)
    det_ref[...] = jnp.sum(correlation * solved, axis=0, keepdims=True) / (rank * level)
    coef_ref[...] = correlation / jnp.sqrt(level)


def local(waveforms, basis, bounds):
    devices = lax.axis_size("chan")
    position = lax.axis_index("chan")
    channels, readings = waveforms.shape
    rank, _, taps = basis.shape
    frequencies = bounds.shape[1]
    full_count = channels * devices
    bin_count = frequencies // devices
    fold = math.gcd(8, bin_count)
    lag_count = readings // devices

    table = jnp.asarray(time_table(frequencies, readings, fold), bf16)
    turned = jnp.swapaxes(basis, 1, 2)
    chunks = bin_count // fold
    if (
        channels % lanes == 0
        and channels > lanes
        and readings % (radix * lanes) == 0
        and chunks > 1
        and half % chunks == 0
        and devices % (half // chunks) == 0
    ):
        detection, coefficients = fused(waveforms, turned, bounds, table, devices, fold)
        return (detection[0], coefficients)

    spectrum = time_spectrum(waveforms, table)
    flat = basis.reshape(rank, channels * taps)
    gram = jnp.einsum("ka,ja->kj", flat, flat, preferred_element_type=f32)
    order = bin_order(frequencies)[0].reshape(-1)
    edges = lax.dynamic_slice_in_dim(bounds[:, order], position * bin_count, bin_count, 1)
    scale = jnp.asarray(np.where(order == 0, 0.5, 1.0) / full_count, f32).reshape(1, -1)
    scale = lax.dynamic_slice_in_dim(scale, position * bin_count, bin_count, 1)
    spectrum = spectrum.reshape(devices, 2 * bin_count, channels)
    gathered = lax.all_to_all(spectrum, "chan", split_axis=0, concat_axis=0, tiled=True)
    passed = filter_plain(gathered, edges, scale, fold)
    filtered = lax.all_to_all(passed, "chan", split_axis=0, concat_axis=0, tiled=True)
    filtered = filtered.reshape(2 * frequencies, channels)
    power, series = power_and_series(turned, filtered, table, readings, fold)
    ahead = 1 + -(-taps // lag_count)
    span = -(-(lag_count + taps) // lanes) * lanes
    power = power.reshape(devices, lag_count)
    windows = jnp.concatenate([jnp.roll(power, -n, axis=0) for n in range(ahead)], axis=1)
    windows = jnp.pad(windows[:, : lag_count + taps], ((0, 0), (0, span - lag_count - taps)))
    gram = jnp.broadcast_to(gram.reshape(1, -1), (devices, rank * rank))
    extra = jnp.concatenate([windows, gram], axis=1)[:, None, :]
    series = series.astype(bf16).reshape(rank, devices, lag_count).transpose(1, 0, 2)
    vmem = pl.BlockSpec(memory_space=pltpu.VMEM)
    detection, coefficients = pl.pallas_call(
        functools.partial(final_kernel, full_count, taps, readings),
        out_shape=(
            jax.ShapeDtypeStruct((1, lag_count), f32),
            jax.ShapeDtypeStruct((rank, lag_count), f32),
        ),
        in_specs=[vmem, vmem],
        out_specs=(vmem, vmem),
        scratch_shapes=[
            pltpu.VMEM(series.shape, bf16),
            pltpu.VMEM(extra.shape, f32),
            pltpu.SemaphoreType.DMA((2, devices)),
            pltpu.SemaphoreType.DMA((2, devices)),
        ],
        compiler_params=pltpu.CompilerParams(
            vmem_limit_bytes=vmem_limit, collective_id=0, has_side_effects=True
        ),
        name="detect",
    )(series, extra)
    return (detection[0], coefficients)


def solution(mesh):
    in_specs = (P("chan", "groups"), P(None, "chan", None), P())
    out_specs = (P(("groups", "chan")), P(None, ("groups", "chan")))
    return jax.shard_map(local, mesh=mesh, in_specs=in_specs, out_specs=out_specs, check_vma=False)
```

```python
import functools
import math

import jax
import jax.numpy as jnp
import numpy as np
from jax import lax
from jax.experimental import pallas as pl
from jax.experimental.pallas import tpu as pltpu
from jax.sharding import PartitionSpec as P

radix = 12
half = radix // 2
lanes = 128
highest = lax.Precision.HIGHEST
bf16 = jnp.bfloat16
f32 = jnp.float32
vmem_limit = 60 * 1024 * 1024


def even_parts(x0, x6, s):
    r = math.sqrt(3.0) / 2.0
    s1, s2, s3, s4, s5 = s
    u, v = x0 + x6, x0 - x6
    e24, d24, e15, d15 = s2 + s4, s2 - s4, s1 + s5, s1 - s5
    even0, odd0 = u + e24, e15 + s3
    even1, odd1 = v + 0.5 * d24, r * d15
    even2, odd2 = u - 0.5 * e24, 0.5 * e15 - s3
    return (
        even0 + odd0,
        even1 + odd1,
        even2 + odd2,
        v - d24,
        even2 - odd2,
        even1 - odd1,
        even0 - odd0,
    )


def odd_parts(d):
    r = math.sqrt(3.0) / 2.0
    d1, d2, d3, d4, d5 = d
    e15, m15 = d1 + d5, d1 - d5
    odd1, even1 = 0.5 * e15 + d3, r * (d2 + d4)
    odd2, even2 = r * m15, r * (d2 - d4)
    return (odd1 + even1, odd2 + even2, e15 - d3, odd2 - even2, odd1 - even1)


def bin_order(frequencies):
    ids = np.arange(frequencies)
    groups = [np.concatenate([ids[ids % radix == 0], ids[ids % radix == half]])]
    signs = [np.ones(frequencies // half)]
    for q in range(1, half):
        plus, minus = ids[ids % radix == q], ids[ids % radix == radix - q]
        groups.append(np.concatenate([plus, minus]))
        signs.append(np.concatenate([np.ones(len(plus)), -np.ones(len(minus))]))
    return np.stack(groups), np.stack(signs)


def time_table(frequencies, readings, fold):
    width = readings // radix
    groups, signs = bin_order(frequencies)
    theta = (groups[:, :, None] * np.arange(width)[None, None, :] % readings) * (
        2.0 * np.pi / readings
    )
    cos, sin = np.cos(theta), np.sin(theta)
    sg = signs[:, :, None]
    real = np.concatenate([cos, -sg * sin], axis=2)
    imag = np.concatenate([-sin, -sg * cos], axis=2)
    first = (groups[0] % radix == 0)[:, None]
    real[0] = np.concatenate([np.where(first, cos[0], 0), np.where(first, 0, cos[0])], axis=1)
    imag[0] = np.concatenate([np.where(first, -sin[0], 0), np.where(first, 0, -sin[0])], axis=1)
    count = groups.shape[1]
    both = np.stack([real, imag], axis=1).reshape(half, 2, count // fold, fold, 2 * width)
    return both.transpose(0, 2, 1, 3, 4).reshape(half, 2 * count, 2 * width)


def row_bins(frequencies, fold):
    order = bin_order(frequencies)[0].reshape(-1, 1, fold)
    return np.broadcast_to(order, (order.shape[0], 2, fold)).reshape(-1)


def butterfly(x_ref, y_ref, start):
    rows, readings = x_ref.shape
    width = readings // radix

    @pl.loop(0, rows // 16)
    def _(r):
        rs = pl.ds(r * 16, 16)
        ys = pl.ds(start + r * 16, 16)
        for b0 in range(0, width, lanes):
            x = [
                x_ref[rs, a * width + b0 : a * width + b0 + lanes].astype(f32)
                for a in range(radix)
            ]
            even = even_parts(x[0], x[half], [x[a] + x[radix - a] for a in range(1, half)])
            odd = odd_parts([x[a] - x[radix - a] for a in range(1, half)])
            left = slice(b0, b0 + lanes)
            right = slice(width + b0, width + b0 + lanes)
            y_ref[0, ys, left] = even[0].astype(bf16)
            y_ref[0, ys, right] = even[half].astype(bf16)
            for q in range(1, half):
                y_ref[q, ys, left] = even[q].astype(bf16)
                y_ref[q, ys, right] = odd[q - 1].astype(bf16)


def spectrum_kernel(blocks, x_ref, table_ref, out_ref, y_ref):
    rows = x_ref.shape[0]
    step = pl.program_id(0)

    @pl.when(step < blocks)
    def _():
        butterfly(x_ref, y_ref, step * rows)

    @pl.when(step >= blocks)
    def _():
        out_ref[...] = lax.dot_general(
            table_ref[0],
            y_ref[step - blocks],
            (((1,), (1,)), ((), ())),
            preferred_element_type=f32,
        ).astype(bf16)


def time_spectrum(waveforms, table):
    channels, readings = waveforms.shape
    block = lanes if channels % lanes == 0 else channels
    blocks = channels // block
    count = table.shape[1]
    group = lambda i: jnp.maximum(i - blocks, 0)
    return pl.pallas_call(
        functools.partial(spectrum_kernel, blocks),
        out_shape=jax.ShapeDtypeStruct((half * count, channels), bf16),
        grid=(blocks + half,),
        in_specs=[
            pl.BlockSpec((block, readings), lambda i: (jnp.minimum(i, blocks - 1), 0)),
            pl.BlockSpec((1,) + table.shape[1:], lambda i: (group(i), 0, 0)),
        ],
        out_specs=pl.BlockSpec((count, channels), lambda i: (group(i), 0)),
        scratch_shapes=[pltpu.VMEM((half, channels, 2 * readings // radix), bf16)],
        compiler_params=pltpu.CompilerParams(vmem_limit_bytes=vmem_limit),
        name="time_spectrum",
    )(waveforms, table)


def series_parts(zr, zs):
    even = even_parts(zr[0], zs[0], zr[1:])
    odd = odd_parts(zs[1:])
    series = [even[0]]
    series += [even[a] + odd[a - 1] for a in range(1, half)]
    series += [even[half]]
    series += [even[a] - odd[a - 1] for a in range(half - 1, 0, -1)]
    return series


def project(b_ref, block, cos, sin):
    taps = cos.shape[0]
    rank = b_ref.shape[0] // taps
    step = math.gcd(4, rank)
    first, second = [], []
    for r0 in range(0, rank, step):
        sums = lax.dot_general(
            b_ref[r0 * taps : (r0 + step) * taps],
            block,
            (((1,), (1,)), ((), ())),
            preferred_element_type=f32,
        )
        for r in range(step):
            member = sums[r * taps : (r + 1) * taps]
            first.append(jnp.sum(member * cos, axis=0, keepdims=True))
            second.append(jnp.sum(member * sin, axis=0, keepdims=True))
    return jnp.concatenate(first, axis=0), jnp.concatenate(second, axis=0)


def member_series(fold, first, second, table):
    rank, count = first.shape
    ids = lax.broadcasted_iota(jnp.int32, first.shape, 1)
    spectra = first + jnp.where(
        (ids // fold) % 2 == 0,
        -pltpu.roll(second, count - fold, 1),
        pltpu.roll(second, fold, 1),
    )
    high = spectra.astype(bf16)
    low = (spectra - high.astype(f32)).astype(bf16)
    both = jnp.dot(jnp.concatenate([high, low], axis=0), table, preferred_element_type=f32)
    return both[:rank] + both[rank:]


def synthesis(block, table):
    return lax.dot_general(block, table, (((0,), (0,)), ((), ())), preferred_element_type=f32)


def series_group(fold, group, block, b_ref, table, cos, sin, z_ref, c_ref):
    z_ref[group] = synthesis(block, table)
    first, second = project(b_ref, block, cos, sin)
    c_ref[group] = member_series(fold, first, second, table)


def sum_power(power_ref, z_ref):
    width = z_ref.shape[2] // 2
    power_ref[...] = jnp.zeros_like(power_ref)

    @pl.loop(0, z_ref.shape[1] // 16)
    def _(r):
        rs = pl.ds(r * 16, 16)
        for b0 in range(0, width, lanes):
            left = slice(b0, b0 + lanes)
            right = slice(width + b0, width + b0 + lanes)
            parts = series_parts(
                [z_ref[g, rs, left] for g in range(half)],
                [z_ref[g, rs, right] for g in range(half)],
            )
            for a, value in enumerate(parts):
                square = value * value
                power_ref[a, :, left] += square[:8] + square[8:]


def series_end(power_ref, out_ref, z_ref, c_ref):
    width = z_ref.shape[2] // 2
    sum_power(power_ref, z_ref)
    parts = series_parts(
        [c_ref[g, :, :width] for g in range(half)],
        [c_ref[g, :, width:] for g in range(half)],
    )
    for a, value in enumerate(parts):
        out_ref[:, a * width : (a + 1) * width] = value


def series_kernel(fold, b_ref, f_ref, t_ref, cos_ref, sin_ref, power_ref, out_ref, z_ref, c_ref):
    group = pl.program_id(0)
    series_group(
        fold, group, f_ref[...], b_ref, t_ref[0], cos_ref[...], sin_ref[...], z_ref, c_ref
    )

    @pl.when(group == half - 1)
    def _():
        series_end(power_ref, out_ref, z_ref, c_ref)


def power_and_series(turned, filtered, table, readings, fold):
    rank, taps, channels = turned.shape
    rows = filtered.shape[0]
    count, width = table.shape[1], table.shape[2] // 2
    bins = row_bins(rows // 2, fold)
    angle = 2.0 * np.pi * (np.arange(taps)[:, None] * bins[None, :] % readings) / readings
    power, series = pl.pallas_call(
        functools.partial(series_kernel, fold),
        out_shape=(
            jax.ShapeDtypeStruct((radix, 8, width), f32),
            jax.ShapeDtypeStruct((rank, readings), f32),
        ),
        grid=(half,),
        in_specs=[
            pl.BlockSpec((rank * taps, channels), lambda i: (0, 0)),
            pl.BlockSpec((count, channels), lambda i: (i, 0)),
            pl.BlockSpec((1,) + table.shape[1:], lambda i: (i, 0, 0)),
            pl.BlockSpec((taps, count), lambda i: (0, i)),
            pl.BlockSpec((taps, count), lambda i: (0, i)),
        ],
        out_specs=(
            pl.BlockSpec((radix, 8, width), lambda i: (0, 0, 0)),
            pl.BlockSpec((rank, readings), lambda i: (0, 0)),
        ),
        scratch_shapes=[
            pltpu.VMEM((half, channels, 2 * width), f32),
            pltpu.VMEM((half, rank, 2 * width), f32),
        ],
        compiler_params=pltpu.CompilerParams(vmem_limit_bytes=vmem_limit),
        name="power_and_series",
    )(
        turned.reshape(rank * taps, channels),
        filtered,
        table,
        jnp.asarray(np.cos(angle), f32),
        jnp.asarray(np.sin(angle), f32),
    )
    return jnp.sum(power, axis=1).reshape(-1), series


def filter_tables(full_count, block_count, parts):
    n2 = lanes
    n1 = full_count // n2
    order = np.arange(n1).reshape(block_count, parts).T.reshape(-1)
    k1, k2, j = np.arange(n1), np.arange(n2), np.arange(n2)
    a1 = 2.0 * np.pi * ((k1[:, None] * order[None, :]) % n1) / n1
    a2 = 2.0 * np.pi * ((j[:, None] * k2[None, :]) % n2) / n2
    at = 2.0 * np.pi * ((k1[:, None] * j[None, :]) % full_count) / full_count
    c1, s1, c2, s2 = np.cos(a1), np.sin(a1), np.cos(a2), np.sin(a2)
    first = np.block([[c1, s1], [-s1, c1]])
    second = np.block([[c2, -s2], [s2, c2]])
    twist = np.stack([np.cos(at), np.sin(at)])
    wave = k1[:, None] + n1 * k2[None, :]
    magnitude = np.minimum(wave, full_count - wave).astype(np.int32)
    return (
        jnp.asarray(first, bf16),
        jnp.asarray(second, bf16),
        jnp.asarray(first.T.copy(), bf16),
        jnp.asarray(second.T.copy(), bf16),
        jnp.asarray(twist, f32),
        jnp.asarray(magnitude),
    )


def filter_chunk(fold, edges, x_ref, w1_ref, w2_ref, v1_ref, v2_ref, tw_ref, mag_ref, o_ref):
    devices = x_ref.shape[0]
    parts = x_ref.shape[2] // lanes
    n1 = mag_ref.shape[0]
    pieces = []
    for ri in range(2):
        for p in range(parts):
            piece = x_ref[:, ri * fold : (ri + 1) * fold, p * lanes : (p + 1) * lanes]
            pieces.append(jnp.swapaxes(piece.astype(f32), 0, 1).astype(bf16))
    stacked = jnp.concatenate(
        [jnp.concatenate([piece[fi] for piece in pieces], axis=0) for fi in range(fold)], axis=1
    )
    waves = jnp.dot(w1_ref[...], stacked, preferred_element_type=f32)
    tc, ts = tw_ref[0], tw_ref[1]
    rows = []
    for fi in range(fold):
        col = slice(fi * lanes, (fi + 1) * lanes)
        re, im = waves[:n1, col], waves[n1:, col]
        rows.append(
            jnp.concatenate([re * tc + im * ts, im * tc - re * ts], axis=1).astype(bf16)
        )
    waves = jnp.dot(jnp.concatenate(rows, axis=0), w2_ref[...], preferred_element_type=f32)
    mag = mag_ref[...]
    rows = []
    for fi in range(fold):
        low, high, _ = edges[fi]
        passing = (mag >= low) & (mag <= high)
        block = waves[fi * n1 : (fi + 1) * n1]
        rows.append(
            jnp.concatenate(
                [
                    jnp.where(passing, block[:, :lanes], 0.0),
                    jnp.where(passing, block[:, lanes:], 0.0),
                ],
                axis=1,
            ).astype(bf16)
        )
    waves = jnp.dot(jnp.concatenate(rows, axis=0), v2_ref[...], preferred_element_type=f32)
    cols = []
    for fi in range(fold):
        block = waves[fi * n1 : (fi + 1) * n1] * edges[fi][2]
        re, im = block[:, :lanes], block[:, lanes:]
        cols.append(
            jnp.concatenate([re * tc - im * ts, im * tc + re * ts], axis=0).astype(bf16)
        )
    out = jnp.dot(v1_ref[...], jnp.concatenate(cols, axis=1), preferred_element_type=f32)
    for ri in range(2):
        for p in range(parts):
            r0 = (ri * parts + p) * devices
            piece = jnp.stack(
                [out[r0 : r0 + devices, fi * lanes : (fi + 1) * lanes] for fi in range(fold)]
            )
            o_ref[:, ri * fold : (ri + 1) * fold, p * lanes : (p + 1) * lanes] = jnp.swapaxes(
                piece, 0, 1
            ).astype(bf16)


def greet(me, devices):
    barrier = pltpu.get_barrier_semaphore()

    @pl.loop(1, devices)
    def _(off):
        pl.semaphore_signal(barrier, inc=1, device_id={"chan": lax.rem(me + off, devices)})

    pl.semaphore_wait(barrier, devices - 1)


def gram_row(b_ref, taps):
    rank = b_ref.shape[0] // taps
    piece = 8 * max(n for n in range(1, 6) if taps % (8 * n) == 0)
    size = rank * piece
    total = jnp.zeros((size, size), f32)
    for j in range(0, taps, piece):
        rows = jnp.concatenate(
            [b_ref[r * taps + j : r * taps + j + piece] for r in range(rank)], axis=0
        )
        total += lax.dot_general(
            rows, rows, (((1,), (1,)), ((), ())), preferred_element_type=f32
        )
    row = lax.broadcasted_iota(jnp.int32, (size, size), 0)
    col = lax.broadcasted_iota(jnp.int32, (size, size), 1)
    total = jnp.where(row % piece == col % piece, total, 0.0)
    left = lax.broadcasted_iota(jnp.int32, (rank, size), 1) // piece
    left = jnp.where(left == lax.broadcasted_iota(jnp.int32, (rank, size), 0), 1.0, 0.0)
    square = rank * rank
    right = lax.broadcasted_iota(jnp.int32, (size, square), 0) // piece
    spread = lax.broadcasted_iota(jnp.int32, (size, square), 1)
    right = jnp.where(right == spread % rank, 1.0, 0.0)
    wide = jnp.dot(
        jnp.dot(left, total, precision=highest, preferred_element_type=f32),
        right,
        precision=highest,
        preferred_element_type=f32,
    )
    keep = lax.broadcasted_iota(jnp.int32, (rank, square), 1) // rank
    keep = keep == lax.broadcasted_iota(jnp.int32, (rank, square), 0)
    return jnp.sum(jnp.where(keep, wide, 0.0), axis=0, keepdims=True)


def inverse(row, rank):
    square = rank * rank
    packed = jnp.broadcast_to(row, (rank, square))
    spread = lax.broadcasted_iota(jnp.int32, packed.shape, 1)
    packed = jnp.where(
        spread // rank == lax.broadcasted_iota(jnp.int32, packed.shape, 0), packed, 0.0
    )
    pick = lax.broadcasted_iota(jnp.int32, (square, rank), 0) % rank
    pick = jnp.where(pick == lax.broadcasted_iota(jnp.int32, pick.shape, 1), 1.0, 0.0)
    gram = jnp.dot(packed, pick, precision=highest)
    ids = lax.broadcasted_iota(jnp.int32, (rank, 1), 0)
    solved = jnp.where(ids == lax.broadcasted_iota(jnp.int32, (rank, rank), 1), 1.0, 0.0)
    for k in range(rank):
        scale = 1.0 / gram[k : k + 1, k : k + 1]
        pivot_g, pivot_s = gram[k : k + 1] * scale, solved[k : k + 1] * scale
        column = gram[:, k : k + 1]
        gram = jnp.where(ids == k, pivot_g, gram - column * pivot_g)
        solved = jnp.where(ids == k, pivot_s, solved - column * pivot_s)
    return solved


def lag_windows(devices, lag_count, taps):
    most = max(d * lag_count % lanes for d in range(devices))
    return -(-(most + lag_count + taps) // lanes)


def fused_kernel(fold, bounds_ref, wave_ref, table_ref, *refs):
    late, (det_ref, coef_ref, *refs) = refs[:9], refs[9:]
    tables, refs = refs[:6], refs[6:]
    wave_buf, y_ref, t_ref, b_ref, cos_ref, sin_ref, *refs = refs
    x_ref, got_ref, mid_ref, out_ref, z_ref, c_ref, *refs = refs
    power_ref, stage_ref, series_ref, row_ref, window_ref, band_ref, *refs = refs
    gram_ref, grams_ref, inv_ref, *refs = refs
    wave_sem, load_sem, sent, came, end_sent, end_came = refs
    chunks, devices, rows, channels = x_ref.shape
    per_chunk = half // chunks
    part = devices // per_chunk
    count = t_ref.shape[1]
    width = t_ref.shape[2] // 2
    readings = radix * width
    rank, lag_count = coef_ref.shape
    taps = b_ref.shape[0] // rank
    bins = count // 2
    full_count = devices * channels
    blocks = channels // lanes
    final = chunks - 1
    early = final * per_chunk
    me = lax.axis_index("chan")
    barrier = pltpu.get_barrier_semaphore()

    def others(body):
        @pl.loop(1, devices)
        def _(off):
            body(lax.rem(me + devices - off, devices))

    def upwards(body):
        @pl.loop(1, devices)
        def _(off):
            body(lax.rem(me + off, devices))

    def remote(src, dst, send_sem, recv_sem, peer):
        return pltpu.make_async_remote_copy(
            src_ref=src,
            dst_ref=dst,
            send_sem=send_sem,
            recv_sem=recv_sem,
            device_id={"chan": peer},
        )

    def arrivals(ref, recv_sem):
        remote(ref, ref, end_sent.at[0], recv_sem, lax.rem(me + 1, devices)).wait_recv()

    def departures(ref, send_sem):
        remote(ref, ref, send_sem, end_came.at[0], lax.rem(me + 1, devices)).wait_send()

    def load_wave(b, slot):
        return pltpu.make_async_copy(
            wave_ref.at[pl.ds(pl.multiple_of(b * lanes, lanes), lanes)],
            wave_buf.at[slot],
            wave_sem.at[slot],
        )

    def load_table(k):
        groups = pl.ds(k * per_chunk, per_chunk)
        return pltpu.make_async_copy(table_ref.at[groups], t_ref.at[groups], load_sem.at[k])

    loads = [
        pltpu.make_async_copy(src, dst, load_sem.at[chunks + n])
        for n, (src, dst) in enumerate(zip(late, (*tables, b_ref, cos_ref, sin_ref)))
    ]

    load_wave(0, 0).start()
    others(lambda peer: pl.semaphore_signal(barrier, inc=1, device_id={"chan": peer}))
    load_table(0).start()
    load_wave(1, 1).start()

    def spectrum(group, block):
        return lax.dot_general(
            t_ref[group], block, (((1,), (1,)), ((), ())), preferred_element_type=f32
        ).astype(bf16)

    @pl.loop(0, blocks)
    def _(b):
        slot = lax.rem(b, 2)
        cs = pl.ds(pl.multiple_of(b * lanes, lanes), lanes)
        load_wave(b, slot).wait()
        butterfly(wave_buf.at[slot], y_ref, b * lanes)

        @pl.when(b + 2 < blocks)
        def _():
            load_wave(b + 2, slot).start()

        @pl.when(b == blocks - 2)
        def _():
            for k in range(1, chunks):
                load_table(k).start()
            for load in loads:
                load.start()

        @pl.when(b == 0)
        def _():
            load_table(0).wait()
            pl.semaphore_wait(barrier, devices - 1)

        for n in range(per_chunk):
            x_ref[0, n * part : (n + 1) * part, :, cs] = spectrum(n, y_ref[n, cs]).reshape(
                part, rows, lanes
            )
        others(
            lambda peer: remote(
                x_ref.at[0, peer, :, cs], got_ref.at[0, me, :, cs], sent.at[0, 0], came.at[0, 0], peer
            ).start()
        )

    got_ref[0, me] = x_ref[0, me]

    @pl.loop(1, chunks)
    def _(k):
        load_table(k).wait()
        for n in range(per_chunk):
            group = k * per_chunk + n
            x_ref[k, n * part : (n + 1) * part] = spectrum(group, y_ref[group]).reshape(
                part, rows, channels
            )
        others(
            lambda peer: remote(
                x_ref.at[k, peer], got_ref.at[k, me], sent.at[0, k], came.at[0, k], peer
            ).start()
        )
        got_ref[k, me] = x_ref[k, me]

    for load in loads:
        load.wait()
    gram_ref[...] = gram_row(b_ref, taps)
    others(
        lambda peer: remote(
            gram_ref, grams_ref.at[me], end_sent.at[0], end_came.at[0], peer
        ).start()
    )
    grams_ref[me] = gram_ref[...]

    @pl.loop(0, chunks)
    def _(k):
        arrivals(got_ref.at[k, : devices - 1], came.at[0, k])
        place = (k * devices + me) * fold
        group, inside = place // bins, place % bins
        side = inside // (bins // 2)
        base = radix * (inside % (bins // 2))
        base += jnp.where(
            group == 0, half * side, jnp.where(side == 0, group, radix - group)
        )
        edges = []
        for fi in range(fold):
            f = base + radix * fi
            scale = jnp.where(f == 0, 0.5 / full_count, 1.0 / full_count)
            edges.append((bounds_ref[0, f], bounds_ref[1, f], scale))
        filter_chunk(fold, edges, got_ref.at[k], *tables, mid_ref.at[k])

        others(
            lambda peer: remote(
                mid_ref.at[k, peer], out_ref.at[k, me], sent.at[1, k], came.at[1, k], peer
            ).start()
        )
        out_ref[k, me] = mid_ref[k, me]

    arrivals(grams_ref.at[: devices - 1], end_came.at[0])
    inv_ref[...] = inverse(jnp.sum(grams_ref[...], axis=0), rank)
    first_lag = me * lag_count
    shift = first_lag % lanes
    row = lax.broadcasted_iota(jnp.int32, band_ref.shape, 0)
    lag = row - lax.broadcasted_iota(jnp.int32, band_ref.shape, 1) - shift
    band_ref[...] = jnp.where((lag >= 0) & (lag < taps), 1.0, 0.0).astype(bf16)

    def returned(k, n):
        return out_ref[k, n * part : (n + 1) * part].reshape(count, channels)

    def member_group(k, n):
        group = k * per_chunk + n
        first, second = project(b_ref, returned(k, n), cos_ref[group], sin_ref[group])
        c_ref[group] = member_series(fold, first, second, t_ref[group])

    @pl.loop(0, final)
    def _(k):
        arrivals(out_ref.at[k, : devices - 1], came.at[1, k])
        for n in range(per_chunk):
            group = k * per_chunk + n
            z_ref[group] = synthesis(returned(k, n), t_ref[group])
            member_group(k, n)

    arrivals(out_ref.at[final, : devices - 1], came.at[1, final])
    for n in range(per_chunk):
        member_group(final, n)

    series = jnp.concatenate(
        series_parts(
            [c_ref[g, :, :width] for g in range(half)],
            [c_ref[g, :, width:] for g in range(half)],
        ),
        axis=1,
    )
    for d in range(devices):
        begin = d * lag_count // lanes * lanes
        off = d * lag_count - begin
        span = -(-(off + lag_count) // lanes) * lanes
        member = series[:, begin : begin + span]
        if off:
            member = pltpu.roll(member, span - off, 1)
        stage_ref[d] = member[:, :lag_count].astype(bf16)
    upwards(
        lambda peer: remote(
            stage_ref.at[peer], series_ref.at[me], end_sent.at[1], end_came.at[1], peer
        ).start()
    )
    series_ref[me] = stage_ref[me]

    for n in range(per_chunk):
        z_ref[early + n] = synthesis(returned(final, n), t_ref[early + n])
    sum_power(power_ref, z_ref)
    power = jnp.sum(power_ref[...], axis=1)
    tiles = width // lanes
    ahead = window_ref.shape[1]
    for a in range(radix):
        for j in range(tiles):
            value = power[a : a + 1, j * lanes : (j + 1) * lanes]
            row_ref[a * tiles + j] = value
            if a * tiles + j < ahead:
                row_ref[radix * tiles + a * tiles + j] = value
    upwards(
        lambda peer: remote(
            row_ref.at[pl.ds(peer * lag_count // lanes, ahead)],
            window_ref.at[me],
            end_sent.at[2],
            end_came.at[2],
            peer,
        ).start()
    )
    window_ref[me] = row_ref[pl.ds(first_lag // lanes, ahead)]

    arrivals(series_ref.at[: devices - 1], end_came.at[1])
    correlation = jnp.sum(series_ref[...].astype(f32), axis=0) * (2.0 / readings)
    solved = jnp.dot(inv_ref[...], correlation, precision=highest)
    numerator = jnp.sum(correlation * solved, axis=0, keepdims=True)
    arrivals(window_ref.at[: devices - 1], end_came.at[2])
    window = jnp.sum(window_ref[...], axis=0)
    window = jnp.concatenate([window[n] for n in range(ahead)], axis=1)
    top = window.astype(bf16).astype(f32)
    middle = (window - top).astype(bf16).astype(f32)
    ids = lax.broadcasted_iota(jnp.int32, (16, window.shape[1]), 0)
    window = jnp.where(
        ids == 0,
        top,
        jnp.where(ids == 1, middle, jnp.where(ids == 2, window - top - middle, 0.0)),
    ).astype(bf16)
    energy = jnp.sum(
        jnp.dot(window, band_ref[...], preferred_element_type=f32), axis=0, keepdims=True
    ) * ((2.0 / readings) ** 2)
    level = energy / (full_count * taps) + 1e-06
    det_ref[...] = numerator / (rank * level)
    coef_ref[...] = correlation / jnp.sqrt(level)

    @pl.loop(0, chunks)
    def _(k):
        departures(x_ref.at[k, : devices - 1], sent.at[0, k])
        departures(mid_ref.at[k, : devices - 1], sent.at[1, k])

    departures(grams_ref.at[: devices - 1], end_sent.at[0])
    departures(stage_ref.at[: devices - 1], end_sent.at[1])
    departures(window_ref.at[: devices - 1], end_sent.at[2])


def fused(waveforms, turned, bounds, table, devices, fold):
    channels, readings = waveforms.shape
    rank, taps, _ = turned.shape
    frequencies = bounds.shape[1]
    count, width = table.shape[1], table.shape[2] // 2
    chunks = frequencies // devices // fold
    per_chunk = half // chunks
    lag_count = readings // devices
    bins = row_bins(frequencies, fold)
    angle = 2.0 * np.pi * (np.arange(taps)[:, None] * bins[None, :] % readings) / readings
    angle = angle.reshape(taps, half, count).transpose(1, 0, 2)
    tables = filter_tables(devices * channels, devices, channels // lanes)
    ahead = lag_windows(devices, lag_count, taps)
    smem = pl.BlockSpec(memory_space=pltpu.SMEM)
    vmem = pl.BlockSpec(memory_space=pltpu.VMEM)
    hbm = pl.BlockSpec(memory_space=pl.ANY)
    exchange = pltpu.VMEM((chunks, devices, 2 * fold, channels), bf16)
    dma = pltpu.SemaphoreType.DMA
    return pl.pallas_call(
        functools.partial(fused_kernel, fold),
        out_shape=(
            pltpu.VMEM((1, lag_count), f32),
            pltpu.VMEM((rank, lag_count), f32),
        ),
        in_specs=[smem] + [hbm] * (5 + len(tables)),
        out_specs=(vmem, vmem),
        scratch_shapes=[
            *(pltpu.VMEM(t.shape, t.dtype) for t in tables),
            pltpu.VMEM((2, lanes, readings), bf16),
            pltpu.VMEM((half, channels, 2 * width), bf16),
            pltpu.VMEM(table.shape, bf16),
            pltpu.VMEM((rank * taps, channels), bf16),
            pltpu.VMEM(angle.shape, f32),
            pltpu.VMEM(angle.shape, f32),
            exchange,
            exchange,
            exchange,
            exchange,
            pltpu.VMEM((half, channels, 2 * width), f32),
            pltpu.VMEM((half, rank, 2 * width), f32),
            pltpu.VMEM((radix, 8, width), f32),
            pltpu.VMEM((devices, rank, lag_count), bf16),
            pltpu.VMEM((devices, rank, lag_count), bf16),
            pltpu.VMEM((readings // lanes + ahead, 1, lanes), f32),
            pltpu.VMEM((devices, ahead, 1, lanes), f32),
            pltpu.VMEM((ahead * lanes, lag_count), bf16),
            pltpu.VMEM((1, rank * rank), f32),
            pltpu.VMEM((devices, 1, rank * rank), f32),
            pltpu.VMEM((rank, rank), f32),
            dma((2,)),
            dma((chunks + 3 + len(tables),)),
            dma((2, chunks)),
            dma((2, chunks)),
            dma((3,)),
            dma((3,)),
        ],
        compiler_params=pltpu.CompilerParams(
            vmem_limit_bytes=vmem_limit, collective_id=1, has_side_effects=True
        ),
        name="detect_all",
    )(
        bounds,
        waveforms,
        table,
        *tables,
        turned.reshape(rank * taps, channels),
        jnp.asarray(np.cos(angle), f32),
        jnp.asarray(np.sin(angle), f32),
    )


def filter_plain(gathered, edges, scale, fold):
    devices, rows, channels = gathered.shape
    full_count = devices * channels
    values = gathered.reshape(devices, rows // (2 * fold), 2, fold, channels)
    values = values.transpose(2, 1, 3, 0, 4).reshape(2, rows // 2, devices, channels)
    d, m = np.arange(devices), np.arange(channels)
    ad = 2.0 * np.pi * (d[:, None] * d[None, :] % devices) / devices
    am = 2.0 * np.pi * (m[:, None] * m[None, :] % channels) / channels
    at = 2.0 * np.pi * (d[:, None] * m[None, :]) / full_count
    wave = d[:, None] + devices * m[None, :]
    magnitude = jnp.asarray(np.minimum(wave, full_count - wave), jnp.int32)[None]

    def turn(layout, angle, pair, sign):
        c, s = jnp.asarray(np.cos(angle), f32), jnp.asarray(sign * np.sin(angle), f32)
        ein = functools.partial(jnp.einsum, layout, precision=highest)
        return ein(c, pair[0]) - ein(s, pair[1]), ein(c, pair[1]) + ein(s, pair[0])

    def twist(pair, sign):
        c, s = jnp.asarray(np.cos(at), f32), jnp.asarray(sign * np.sin(at), f32)
        return c * pair[0] - s * pair[1], c * pair[1] + s * pair[0]

    pair = (values[0].astype(f32), values[1].astype(f32))
    pair = twist(turn("kp,fpm->fkm", ad, pair, -1.0), -1.0)
    pair = turn("mn,fkm->fkn", am, pair, -1.0)
    passing = (magnitude >= edges[0][:, None, None]) & (magnitude <= edges[1][:, None, None])
    pair = tuple(jnp.where(passing, part, 0.0) for part in pair)
    pair = twist(turn("mn,fkn->fkm", am, pair, 1.0), 1.0)
    pair = turn("kp,fkm->fpm", ad, pair, 1.0)
    out = (jnp.stack(pair) * scale[0][None, :, None, None]).astype(bf16)
    out = out.reshape(2, rows // (2 * fold), fold, devices, channels).transpose(3, 1, 0, 2, 4)
    return out.reshape(devices, rows, channels)


def final_kernel(
    full_count, taps, readings, series_ref, extra_ref, det_ref, coef_ref, got_ref, more_ref, sent, came
):
    devices, rank, lag_count = series_ref.shape
    square = rank * rank
    span = extra_ref.shape[2] - square
    me = lax.axis_index("chan")
    greet(me, devices)

    def copies(peer, slot):
        pair = ((series_ref, got_ref), (extra_ref, more_ref))
        return [
            pltpu.make_async_remote_copy(
                src_ref=src.at[peer],
                dst_ref=dst.at[slot],
                send_sem=sent.at[n, peer],
                recv_sem=came.at[n, slot],
                device_id={"chan": peer},
            )
            for n, (src, dst) in enumerate(pair)
        ]

    @pl.loop(1, devices)
    def _(off):
        for copy in copies(lax.rem(me + off, devices), me):
            copy.start()

    got_ref[me] = series_ref[me]
    more_ref[me] = extra_ref[me]

    @pl.loop(1, devices)
    def _(off):
        peer = lax.rem(me + off, devices)
        for copy in copies(peer, peer):
            copy.wait()

    correlation = jnp.sum(got_ref[...].astype(f32), axis=0) * (2.0 / readings)
    extra = jnp.sum(more_ref[...], axis=0)
    window = extra[:, :span]
    packed = jnp.broadcast_to(extra[:, span:], (rank, square))
    spread = lax.broadcasted_iota(jnp.int32, packed.shape, 1)
    packed = jnp.where(
        spread // rank == lax.broadcasted_iota(jnp.int32, packed.shape, 0), packed, 0.0
    )
    pick = lax.broadcasted_iota(jnp.int32, (square, rank), 0) % rank
    pick = jnp.where(pick == lax.broadcasted_iota(jnp.int32, pick.shape, 1), 1.0, 0.0)
    gram = jnp.dot(packed, pick, precision=highest)
    row = lax.broadcasted_iota(jnp.int32, (window.shape[1], lag_count), 0)
    lag = row - lax.broadcasted_iota(jnp.int32, row.shape, 1)
    band = jnp.where((lag >= 0) & (lag < taps), 1.0, 0.0)
    energy = jnp.dot(
        jnp.broadcast_to(window, (8, window.shape[1])), band, precision=highest
    )[:1] * (2.0 / readings) ** 2
    level = energy / (full_count * taps) + 1e-06
    solved = correlation
    ids = lax.broadcasted_iota(jnp.int32, (rank, 1), 0)
    for k in range(rank):
        inverse = 1.0 / gram[k : k + 1, k : k + 1]
        pivot_g, pivot_c = gram[k : k + 1] * inverse, solved[k : k + 1] * inverse
        column = gram[:, k : k + 1]
        gram = jnp.where(ids == k, pivot_g, gram - column * pivot_g)
        solved = jnp.where(ids == k, pivot_c, solved - column * pivot_c)
    det_ref[...] = jnp.sum(correlation * solved, axis=0, keepdims=True) / (rank * level)
    coef_ref[...] = correlation / jnp.sqrt(level)


def local(waveforms, basis, bounds):
    devices = lax.axis_size("chan")
    position = lax.axis_index("chan")
    channels, readings = waveforms.shape
    rank, _, taps = basis.shape
    frequencies = bounds.shape[1]
    full_count = channels * devices
    bin_count = frequencies // devices
    fold = math.gcd(8, bin_count)
    lag_count = readings // devices

    table = jnp.asarray(time_table(frequencies, readings, fold), bf16)
    turned = jnp.swapaxes(basis, 1, 2)
    chunks = bin_count // fold
    if (
        channels % lanes == 0
        and channels > lanes
        and readings % (radix * lanes) == 0
        and chunks > 1
        and half % chunks == 0
        and devices % (half // chunks) == 0
    ):
        detection, coefficients = fused(waveforms, turned, bounds, table, devices, fold)
        return (detection[0], coefficients)

    spectrum = time_spectrum(waveforms, table)
    flat = basis.reshape(rank, channels * taps)
    gram = jnp.einsum("ka,ja->kj", flat, flat, preferred_element_type=f32)
    order = bin_order(frequencies)[0].reshape(-1)
    edges = lax.dynamic_slice_in_dim(bounds[:, order], position * bin_count, bin_count, 1)
    scale = jnp.asarray(np.where(order == 0, 0.5, 1.0) / full_count, f32).reshape(1, -1)
    scale = lax.dynamic_slice_in_dim(scale, position * bin_count, bin_count, 1)
    spectrum = spectrum.reshape(devices, 2 * bin_count, channels)
    gathered = lax.all_to_all(spectrum, "chan", split_axis=0, concat_axis=0, tiled=True)
    passed = filter_plain(gathered, edges, scale, fold)
    filtered = lax.all_to_all(passed, "chan", split_axis=0, concat_axis=0, tiled=True)
    filtered = filtered.reshape(2 * frequencies, channels)
    power, series = power_and_series(turned, filtered, table, readings, fold)
    ahead = 1 + -(-taps // lag_count)
    span = -(-(lag_count + taps) // lanes) * lanes
    power = power.reshape(devices, lag_count)
    windows = jnp.concatenate([jnp.roll(power, -n, axis=0) for n in range(ahead)], axis=1)
    windows = jnp.pad(windows[:, : lag_count + taps], ((0, 0), (0, span - lag_count - taps)))
    gram = jnp.broadcast_to(gram.reshape(1, -1), (devices, rank * rank))
    extra = jnp.concatenate([windows, gram], axis=1)[:, None, :]
    series = series.astype(bf16).reshape(rank, devices, lag_count).transpose(1, 0, 2)
    vmem = pl.BlockSpec(memory_space=pltpu.VMEM)
    detection, coefficients = pl.pallas_call(
        functools.partial(final_kernel, full_count, taps, readings),
        out_shape=(
            jax.ShapeDtypeStruct((1, lag_count), f32),
            jax.ShapeDtypeStruct((rank, lag_count), f32),
        ),
        in_specs=[vmem, vmem],
        out_specs=(vmem, vmem),
        scratch_shapes=[
            pltpu.VMEM(series.shape, bf16),
            pltpu.VMEM(extra.shape, f32),
            pltpu.SemaphoreType.DMA((2, devices)),
            pltpu.SemaphoreType.DMA((2, devices)),
        ],
        compiler_params=pltpu.CompilerParams(
            vmem_limit_bytes=vmem_limit, collective_id=0, has_side_effects=True
        ),
        name="detect",
    )(series, extra)
    return (detection[0], coefficients)


def solution(mesh):
    in_specs = (P("chan", "groups"), P(None, "chan", None), P())
    out_specs = (P(("groups", "chan")), P(None, ("groups", "chan")))
    return jax.shard_map(local, mesh=mesh, in_specs=in_specs, out_specs=out_specs, check_vma=False)
```
